32 devices in a mesh: uly: 8 (over z, y), blk: 4 (over x, core).
Axes of the slice: x: 2, y: 2, z: 4, core: 2. Of those that a mesh axis runs over, the one named last changes fastest.
Arguments:
- queries: bfloat16 [2048, 2048], P(('blk', 'uly')), may hold values from -20 to 20
- keys: bfloat16 [2048, 2048], P(('blk', 'uly')), may hold values from -20 to 20
- values: bfloat16 [2048, 2048], P(('blk', 'uly')), may hold values from -6 to 6
- block_list: int32 [32, 16, 16], P('uly', 'blk'), may hold values from -1 to 15, as said below
Outputs:
- attended: bfloat16 [2048, 2048], P(('blk', 'uly'))
The draws below stay inside these ranges and needn't reach their ends.
Inputs may be any that keep to these rules, and one draw needn't show every extreme that they name: block_list[h, b, 0] = b; every other entry is -1 (an empty slot) or a block below b, and the blocks named in one list are distinct.
All inputs are finite; a program needn't handle non-finite values.
Results may differ from the reference program's by a relative error of at most 0.0045.
Values may be sent and summed in bfloat16 or wider, within the bound.
No kernel may reach another device: no remote copies, remote signals or barrier semaphores. Data moves between devices by JAX's collectives and lax.ppermute only.
A program may use at most 64 MiB of HBM per device.

```python
import jax
import jax.numpy as jnp
from jax import lax

HEADS = 32
WIDTH = 2048
BLOCK = 128
SLOTS = 16
QGROUP = 2
SEQ = 2048
NBLOCKS = 16


def pair_base(key):
    query_draw = jax.random.normal(jax.random.fold_in(key, 101), (SEQ, WIDTH), jnp.float32)
    key_draw = jax.random.normal(jax.random.fold_in(key, 102), (SEQ, WIDTH), jnp.float32)
    query_draw = jnp.clip(query_draw, -6.0, 6.0)
    key_draw = jnp.clip(key_draw, -6.0, 6.0)
    return (query_draw, key_draw)


def draw_queries(key, part):
    return pair_base(key)[0].astype(jnp.bfloat16)


def draw_keys(key, part):
    return pair_base(key)[1].astype(jnp.bfloat16)


def draw_block_list(key, part):
    pattern_kind = jax.random.randint(jax.random.fold_in(key, 1), (HEADS,), 0, 3)
    counts = jax.random.randint(jax.random.fold_in(key, 2), (HEADS,), 2, SLOTS + 1)
    query_block = jnp.arange(NBLOCKS, dtype=jnp.int32)[:, None]
    slot_index = jnp.arange(SLOTS, dtype=jnp.int32)[None, :]
    window = jnp.where(query_block - slot_index >= 0, query_block - slot_index, -1)
    sink_entry = jnp.where(slot_index == 0, query_block, jnp.where(slot_index == 1, 0, query_block - slot_index + 1))
    sink_valid = (slot_index == 0) | (slot_index == 1) & (query_block >= 1) | (slot_index >= 2) & (query_block - slot_index + 1 >= 1)
    sink_list = jnp.where(sink_valid, sink_entry, -1)
    candidate = jnp.arange(NBLOCKS, dtype=jnp.int32)
    ranking = jax.random.randint(jax.random.fold_in(key, 3), (HEADS, NBLOCKS, NBLOCKS), 0, 1048576) * NBLOCKS + candidate[None, None, :]
    ranking = jnp.where((candidate[None, :] < query_block)[None, :, :], ranking, -1)
    best_values, chosen_index = lax.top_k(ranking, SLOTS - 1)
    picked = jnp.where(best_values >= 0, chosen_index, -1)
    diagonal = jnp.broadcast_to(query_block[None, :, :], (HEADS, NBLOCKS, 1))
    retrieval = jnp.concatenate([diagonal, picked], axis=2)
    kind_wide = pattern_kind[:, None, None]
    pattern = jnp.where(kind_wide == 0, sink_list[None], jnp.where(kind_wide == 1, window[None], retrieval))
    pattern = jnp.where(slot_index[None, :, :] < counts[:, None, None], pattern, -1)
    return pattern.astype(jnp.int32)


def levels(own_key, extent, split, smallest, top_value):
    level = 1.0
    for axis_at, shards_of in split:
        draws = jax.random.uniform(jax.random.fold_in(jax.random.fold_in(own_key, 6), axis_at), (shards_of,), jnp.float32, smallest / len(split), top_value / len(split))
        level = level * jnp.repeat(jnp.exp(draws), extent[axis_at] // shards_of).reshape((-1,) + (1,) * (len(extent) - 1 - axis_at))
    return level


def gaussian(own_key, dims, scale, bound, cuts=(), held_as=jnp.bfloat16):
    entries = scale * jax.random.normal(own_key, dims, jnp.float32)
    if cuts:
        entries = entries * levels(own_key, dims, cuts, -0.22, 0.18)
    return jnp.clip(entries, -bound, bound).astype(held_as)


def setup_inputs(seed: int = 0) -> dict:
    seeds = jax.random.split(jax.random.key(seed), 5)
    return {
        "queries": draw_queries(jax.random.fold_in(seeds[4], 71), 0),
        "keys": draw_keys(jax.random.fold_in(seeds[4], 71), 0),
        "values": gaussian(seeds[2], (SEQ, WIDTH), 1.0, 6.0, ((0, 32),)),
        "block_list": draw_block_list(jax.random.fold_in(seeds[4], 71), 0),
    }


def attend_block(query_group, key_slots, value_slots, chosen, query_block):
    scale = query_group.shape[-1] ** -0.5
    scores = jnp.einsum("abd,asjd->absj", query_group.astype(jnp.float32), key_slots.astype(jnp.float32)) * scale
    positions = jnp.arange(BLOCK, dtype=jnp.int32)
    query_pos = query_block[:, None] * BLOCK + positions[None, :]
    key_pos = jnp.maximum(chosen, 0)[:, :, None] * BLOCK + positions[None, None, :]
    allowed = (chosen[:, None, :, None] >= 0) & (key_pos[:, None, :, :] <= query_pos[:, :, None, None])
    scores = jnp.where(allowed, scores, -1e30)
    row_max = jnp.max(scores, axis=(2, 3), keepdims=True)
    weights = jnp.where(allowed, jnp.exp(scores - row_max), 0.0)
    denominator = jnp.sum(weights, axis=(2, 3))
    rounded = weights.astype(jnp.bfloat16)
    summed = jnp.einsum("absj,asjd->abd", rounded.astype(jnp.float32), value_slots.astype(jnp.float32))
    return (summed / denominator[:, :, None]).astype(jnp.bfloat16)


def reference(queries, keys, values, block_list):
    heads = block_list.shape[0]
    nblocks = block_list.shape[1]
    head_dim = queries.shape[1] // heads
    groups_per_head = nblocks // QGROUP

    def by_heads(token_rows):
        return token_rows.reshape(nblocks, BLOCK, heads, head_dim).transpose(2, 0, 1, 3)

    query_heads = by_heads(queries)
    key_heads = by_heads(keys)
    value_heads = by_heads(values)

    def attend_item(flat_index):
        head_index = flat_index // groups_per_head
        first = (flat_index % groups_per_head) * QGROUP
        query_head = lax.dynamic_index_in_dim(query_heads, head_index, 0, keepdims=False)
        key_head = lax.dynamic_index_in_dim(key_heads, head_index, 0, keepdims=False)
        value_head = lax.dynamic_index_in_dim(value_heads, head_index, 0, keepdims=False)
        list_head = lax.dynamic_index_in_dim(block_list, head_index, 0, keepdims=False)
        query_group = lax.dynamic_slice_in_dim(query_head, first, QGROUP, 0)
        chosen = lax.dynamic_slice_in_dim(list_head, first, QGROUP, 0)
        safe = jnp.maximum(chosen, 0).astype(jnp.int32)
        key_slots = jnp.take(key_head, safe, axis=0)
        value_slots = jnp.take(value_head, safe, axis=0)
        query_block = (first + jnp.arange(QGROUP, dtype=jnp.int32)).astype(jnp.int32)
        return attend_block(query_group, key_slots, value_slots, chosen, query_block)

    result = lax.map(attend_item, jnp.arange(heads * groups_per_head, dtype=jnp.int32))
    result = result.reshape(heads, nblocks * BLOCK, head_dim).transpose(1, 0, 2)
    return result.reshape(nblocks * BLOCK, heads * head_dim)
```

```python
import functools
import math

import jax
import jax.numpy as jnp
from jax import lax
from jax.experimental import pallas as pl
from jax.experimental.pallas import tpu as pltpu
from jax.sharding import PartitionSpec as P

BLOCK = 128
QGROUP = 2
LANES = 128
NEG = -1e30
EVERY = ("blk", "uly")


def head_major(token_rows, heads_local, head_dim):
    return token_rows.reshape(token_rows.shape[0] // BLOCK, BLOCK, heads_local, head_dim).transpose(
        2, 0, 1, 3
    )


def select_blocks(source, chosen):
    return jnp.take(source, chosen, axis=0)


def attend_block(operand):
    query_group, key_slots, value_slots, chosen, query_block = operand
    scale = query_group.shape[-1] ** (-0.5)
    scores = (
        jnp.einsum("abd,asjd->absj", query_group, key_slots, preferred_element_type=jnp.float32)
        * scale
    )
    positions = jnp.arange(BLOCK, dtype=jnp.int32)
    query_pos = query_block[:, None] * BLOCK + positions[None, :]
    key_pos = jnp.maximum(chosen, 0)[:, :, None] * BLOCK + positions[None, None, :]
    allowed = (chosen[:, None, :, None] >= 0) & (
        key_pos[:, None, :, :] <= query_pos[:, :, None, None]
    )
    scores = jnp.where(allowed, scores, -1e30)
    row_max = jnp.max(scores, axis=(2, 3), keepdims=True)
    weights = jnp.where(allowed, jnp.exp(scores - row_max), 0.0)
    denominator = jnp.sum(weights, axis=(2, 3))
    rounded = weights.astype(jnp.bfloat16)
    summed = jnp.einsum("absj,asjd->abd", rounded, value_slots, preferred_element_type=jnp.float32)
    return (summed / denominator[:, :, None]).astype(jnp.bfloat16)


def by_context(queries, keys, values, block_list):
    heads_local = block_list.shape[0]
    blocks_dev = block_list.shape[1]
    slot_count = block_list.shape[2]
    head_dim = queries.shape[1] // (heads_local * lax.axis_size("uly"))
    first_block = lax.axis_index("blk") * blocks_dev
    query_rows, key_rows, value_rows = (
        lax.all_to_all(queries, "uly", split_axis=1, concat_axis=0, tiled=True),
        lax.all_to_all(keys, "uly", split_axis=1, concat_axis=0, tiled=True),
        lax.all_to_all(values, "uly", split_axis=1, concat_axis=0, tiled=True),
    )
    keys_all = lax.all_gather(key_rows, "blk", axis=0, tiled=True)
    values_all = lax.all_gather(value_rows, "blk", axis=0, tiled=True)
    chosen = jnp.maximum(block_list, 0)
    key_slots = jax.vmap(select_blocks)(head_major(keys_all, heads_local, head_dim), chosen)
    value_slots = jax.vmap(select_blocks)(head_major(values_all, heads_local, head_dim), chosen)
    groups = heads_local * blocks_dev // QGROUP
    query_heads = head_major(query_rows, heads_local, head_dim).reshape(
        groups, QGROUP, BLOCK, head_dim
    )
    key_groups = key_slots.reshape(groups, QGROUP, slot_count, BLOCK, head_dim)
    value_groups = value_slots.reshape(groups, QGROUP, slot_count, BLOCK, head_dim)
    list_groups = block_list.reshape(groups, QGROUP, slot_count)
    block_numbers = first_block + jnp.arange(blocks_dev, dtype=jnp.int32)
    block_groups = jnp.broadcast_to(block_numbers[None, :], (heads_local, blocks_dev)).reshape(
        groups, QGROUP
    )
    result = lax.map(
        attend_block, (query_heads, key_groups, value_groups, list_groups, block_groups)
    )
    result = result.reshape(heads_local, blocks_dev * BLOCK, head_dim).transpose(1, 0, 2)
    result = result.reshape(blocks_dev * BLOCK, heads_local * head_dim)
    return lax.all_to_all(result, "uly", split_axis=0, concat_axis=1, tiled=True)


def lane_of(shape):
    return lax.broadcasted_iota(jnp.int32, shape, len(shape) - 1)


def pack_kernel(nu, nb, q_ref, k_ref, v_ref, list_ref, out_ref, *rest):
    bias_refs, bias = rest[:nb], rest[nb]
    rows = q_ref.shape[0]
    half, hd = rows // 2, LANES // 2
    low = lane_of((rows, LANES)) < hd
    low_half = lane_of((half, LANES)) < hd
    for pair in range(q_ref.shape[1] // LANES):
        cols = slice(pair * LANES, (pair + 1) * LANES)
        q, k, v = q_ref[:, cols], k_ref[:, cols], v_ref[:, cols]
        k_turned, v_turned = pltpu.roll(k, hd, 1), pltpu.roll(v, hd, 1)
        q_turned = pltpu.roll(q, hd, 1)
        for odd in range(2):
            head = 2 * pair + odd
            dest = (head % nb) * nu + head // nb
            if odd:
                kv = jnp.where(low, k_turned, v)
                qq = jnp.where(low_half, q_turned[:half], q[half:])
            else:
                kv = jnp.where(low, k, v_turned)
                qq = jnp.where(low_half, q[:half], q_turned[half:])
            out_ref[dest, :rows, :] = kv
            out_ref[dest, rows:, :] = qq
    listed = list_ref[...]
    lane = lane_of((listed.shape[0], LANES)) - hd
    allowed = jnp.zeros((listed.shape[0], LANES), jnp.bool_)
    for slot in range(listed.shape[1]):
        allowed = allowed | (listed[:, slot : slot + 1] == lane)
    blocks = listed.shape[0] // nb
    all_bias = jnp.where(allowed, 0.0, NEG)
    for head in range(nb):
        bias[head] = all_bias[head * blocks : (head + 1) * blocks]
    me = lax.axis_index("blk")
    for step in range(nb):
        bias_refs[step][...] = bias[lax.rem(me + step, nb)]


def attend_kernel(nb, scale, g_ref, *rest):
    bias_refs, (out_ref, qx, kx, vx, bias) = rest[:nb], rest[nb:]
    chunks, packed, _ = g_ref.shape
    rows = packed * 2 // 3
    half, hd = rows // 2, LANES // 2
    blocks = chunks * rows // BLOCK
    here = blocks // nb
    me = lax.axis_index("blk")
    for step in range(nb):
        bias[lax.rem(me + nb - step, nb)] = bias_refs[step][...]
    lane = lane_of((rows, LANES))
    low = lane < hd
    low_half = lane_of((half, LANES)) < hd
    one = jnp.ones((rows, LANES), jnp.bfloat16)
    for t in range(chunks):
        b = t * rows // BLOCK
        kv = g_ref[t, :rows, :]
        q = g_ref[t, rows:, :]
        row = jnp.broadcast_to(bias[b // here, b % here : b % here + 1, :], (half, LANES))
        row = row.astype(jnp.bfloat16)
        at = t * rows
        kx[at : at + rows, :] = jnp.where(low, kv, (lane == hd + b).astype(jnp.bfloat16))
        vx[at : at + rows, :] = jnp.where(low, one, kv)
        qx[at : at + half, :] = jnp.where(low_half, q, row)
        qx[at + half : at + rows, :] = jnp.where(low_half, pltpu.roll(q, hd, 1), row)
    group = QGROUP * BLOCK
    later = lax.broadcasted_iota(jnp.int32, (group, group), 1) > lax.broadcasted_iota(
        jnp.int32, (group, group), 0
    )
    factor = scale * math.log2(math.e)
    for g in range(blocks // QGROUP):
        at = g * group
        query = qx[at : at + group, :]
        scores = []
        for c in range(g + 1):
            s = lax.dot_general(
                query,
                kx[c * group : (c + 1) * group, :],
                (((1,), (1,)), ((), ())),
                preferred_element_type=jnp.float32,
            )
            scores.append(jnp.where(later, NEG, s) if c == g else s)
        top = functools.reduce(jnp.maximum, scores)
        top = jnp.max(top, axis=1, keepdims=True)
        total = jnp.zeros((group, LANES), jnp.float32)
        for c in range(g + 1):
            weight = jnp.exp2((scores[c] - top) * factor).astype(jnp.bfloat16)
            total += jnp.dot(
                weight, vx[c * group : (c + 1) * group, :], preferred_element_type=jnp.float32
            )
        turned = pltpu.roll(total, hd, 1)
        for i in range(group // rows):
            a, m, e = i * rows, i * rows + half, (i + 1) * rows
            upper = jnp.where(low_half, turned[a:m], total[m:e])
            lower = jnp.where(low_half, total[a:m], turned[m:e])
            out_ref[at // rows + i] = (upper / lower).astype(jnp.bfloat16)


def unpack_kernel(nu, nb, g_ref, out_ref):
    half, hd = g_ref.shape[1], LANES // 2
    low = lane_of((half, LANES)) < hd
    for pair in range(out_ref.shape[1] // LANES):
        cols = slice(pair * LANES, (pair + 1) * LANES)
        even, odd = 2 * pair, 2 * pair + 1
        a = g_ref[(even % nb) * nu + even // nb]
        b = g_ref[(odd % nb) * nu + odd // nb]
        out_ref[:half, cols] = jnp.where(low, a, pltpu.roll(b, hd, 1))
        out_ref[half:, cols] = jnp.where(low, pltpu.roll(a, hd, 1), b)


def by_head(queries, keys, values, block_list):
    nu, nb = lax.axis_size("uly"), lax.axis_size("blk")
    count = nu * nb
    rows, width = queries.shape
    heads_local, here, slots = block_list.shape
    head_dim = width // (heads_local * nu)
    blocks = here * nb
    vmem = pl.BlockSpec(memory_space=pltpu.VMEM)
    small = jax.ShapeDtypeStruct((here, LANES), jnp.float32)
    packed, *bias = pl.pallas_call(
        functools.partial(pack_kernel, nu, nb),
        out_shape=(jax.ShapeDtypeStruct((count, rows * 3 // 2, LANES), jnp.bfloat16),)
        + (small,) * nb,
        in_specs=[vmem] * 4,
        out_specs=(vmem,) * (nb + 1),
        scratch_shapes=[pltpu.VMEM((nb, here, LANES), jnp.float32)],
        cost_estimate=pl.CostEstimate(
            flops=4 * rows * width, bytes_accessed=12 * rows * width, transcendentals=0
        ),
    )(queries, keys, values, block_list.reshape(heads_local * here, slots))
    whole = lax.all_to_all(packed, EVERY, split_axis=0, concat_axis=0)
    moved = [bias[0]] + [
        lax.ppermute(bias[step], "blk", [(i, (i + step) % nb) for i in range(nb)])
        for step in range(1, nb)
    ]
    tokens = count * rows
    attended = pl.pallas_call(
        functools.partial(attend_kernel, nb, head_dim**-0.5),
        out_shape=jax.ShapeDtypeStruct((count, rows // 2, LANES), jnp.bfloat16),
        in_specs=[vmem] * (nb + 1),
        out_specs=vmem,
        scratch_shapes=[pltpu.VMEM((tokens, LANES), jnp.bfloat16)] * 3
        + [pltpu.VMEM((nb, here, LANES), jnp.float32)],
        cost_estimate=pl.CostEstimate(
            flops=4 * tokens * tokens // 2 * LANES,
            bytes_accessed=4 * tokens * LANES * 2,
            transcendentals=tokens * tokens // 2,
        ),
    )(whole, *moved)
    back = lax.all_to_all(attended, EVERY, split_axis=0, concat_axis=0)
    return pl.pallas_call(
        functools.partial(unpack_kernel, nu, nb),
        out_shape=jax.ShapeDtypeStruct((rows, width), jnp.bfloat16),
        in_specs=[vmem],
        out_specs=vmem,
        cost_estimate=pl.CostEstimate(
            flops=2 * rows * width, bytes_accessed=4 * rows * width, transcendentals=0
        ),
    )(back)


def local(queries, keys, values, block_list):
    nu, nb = lax.axis_size("uly"), lax.axis_size("blk")
    rows, width = queries.shape
    heads_local, here, _ = block_list.shape
    head_dim = width // (heads_local * nu)
    blocks = here * nb
    one_head = (
        heads_local == nb
        and 2 * head_dim == LANES
        and blocks <= LANES // 2
        and blocks % QGROUP == 0
        and BLOCK % rows == 0
        and rows % 32 == 0
    )
    return (by_head if one_head else by_context)(queries, keys, values, block_list)


def solution(mesh):
    placed = (
        P(("blk", "uly"), None),
        P(("blk", "uly"), None),
        P(("blk", "uly"), None),
        P("uly", "blk", None),
    )
    return jax.shard_map(
        local, mesh=mesh, in_specs=placed, out_specs=P(("blk", "uly"), None), check_vma=False
    )
```

```python
import functools
import math

import jax
import jax.numpy as jnp
from jax import lax
from jax.experimental import pallas as pl
from jax.experimental.pallas import tpu as pltpu
from jax.sharding import PartitionSpec as P

BLOCK = 128
QGROUP = 2
LANES = 128
NEG = -1e30
EVERY = ("blk", "uly")


def head_major(token_rows, heads_local, head_dim):
    return token_rows.reshape(token_rows.shape[0] // BLOCK, BLOCK, heads_local, head_dim).transpose(
        2, 0, 1, 3
    )


def select_blocks(source, chosen):
    return jnp.take(source, chosen, axis=0)


def attend_block(operand):
    query_group, key_slots, value_slots, chosen, query_block = operand
    scale = query_group.shape[-1] ** (-0.5)
    scores = (
        jnp.einsum("abd,asjd->absj", query_group, key_slots, preferred_element_type=jnp.float32)
        * scale
    )
    positions = jnp.arange(BLOCK, dtype=jnp.int32)
    query_pos = query_block[:, None] * BLOCK + positions[None, :]
    key_pos = jnp.maximum(chosen, 0)[:, :, None] * BLOCK + positions[None, None, :]
    allowed = (chosen[:, None, :, None] >= 0) & (
        key_pos[:, None, :, :] <= query_pos[:, :, None, None]
    )
    scores = jnp.where(allowed, scores, -1e30)
    row_max = jnp.max(scores, axis=(2, 3), keepdims=True)
    weights = jnp.where(allowed, jnp.exp(scores - row_max), 0.0)
    denominator = jnp.sum(weights, axis=(2, 3))
    rounded = weights.astype(jnp.bfloat16)
    summed = jnp.einsum("absj,asjd->abd", rounded, value_slots, preferred_element_type=jnp.float32)
    return (summed / denominator[:, :, None]).astype(jnp.bfloat16)


def by_context(queries, keys, values, block_list):
    heads_local = block_list.shape[0]
    blocks_dev = block_list.shape[1]
    slot_count = block_list.shape[2]
    head_dim = queries.shape[1] // (heads_local * lax.axis_size("uly"))
    first_block = lax.axis_index("blk") * blocks_dev
    query_rows, key_rows, value_rows = (
        lax.all_to_all(queries, "uly", split_axis=1, concat_axis=0, tiled=True),
        lax.all_to_all(keys, "uly", split_axis=1, concat_axis=0, tiled=True),
        lax.all_to_all(values, "uly", split_axis=1, concat_axis=0, tiled=True),
    )
    keys_all = lax.all_gather(key_rows, "blk", axis=0, tiled=True)
    values_all = lax.all_gather(value_rows, "blk", axis=0, tiled=True)
    chosen = jnp.maximum(block_list, 0)
    key_slots = jax.vmap(select_blocks)(head_major(keys_all, heads_local, head_dim), chosen)
    value_slots = jax.vmap(select_blocks)(head_major(values_all, heads_local, head_dim), chosen)
    groups = heads_local * blocks_dev // QGROUP
    query_heads = head_major(query_rows, heads_local, head_dim).reshape(
        groups, QGROUP, BLOCK, head_dim
    )
    key_groups = key_slots.reshape(groups, QGROUP, slot_count, BLOCK, head_dim)
    value_groups = value_slots.reshape(groups, QGROUP, slot_count, BLOCK, head_dim)
    list_groups = block_list.reshape(groups, QGROUP, slot_count)
    block_numbers = first_block + jnp.arange(blocks_dev, dtype=jnp.int32)
    block_groups = jnp.broadcast_to(block_numbers[None, :], (heads_local, blocks_dev)).reshape(
        groups, QGROUP
    )
    result = lax.map(
        attend_block, (query_heads, key_groups, value_groups, list_groups, block_groups)
    )
    result = result.reshape(heads_local, blocks_dev * BLOCK, head_dim).transpose(1, 0, 2)
    result = result.reshape(blocks_dev * BLOCK, heads_local * head_dim)
    return lax.all_to_all(result, "uly", split_axis=0, concat_axis=1, tiled=True)


def lane_of(shape):
    return lax.broadcasted_iota(jnp.int32, shape, len(shape) - 1)


def pack_kernel(nu, nb, q_ref, k_ref, v_ref, list_ref, out_ref, *rest):
    bias_refs, bias = rest[:nb], rest[nb]
    rows = q_ref.shape[0]
    half, hd = rows // 2, LANES // 2
    low = lane_of((rows, LANES)) < hd
    low_half = lane_of((half, LANES)) < hd
    for pair in range(q_ref.shape[1] // LANES):
        cols = slice(pair * LANES, (pair + 1) * LANES)
        q, k, v = q_ref[:, cols], k_ref[:, cols], v_ref[:, cols]
        k_turned, v_turned = pltpu.roll(k, hd, 1), pltpu.roll(v, hd, 1)
        q_turned = pltpu.roll(q, hd, 1)
        for odd in range(2):
            head = 2 * pair + odd
            dest = (head % nb) * nu + head // nb
            if odd:
                kv = jnp.where(low, k_turned, v)
                qq = jnp.where(low_half, q_turned[:half], q[half:])
            else:
                kv = jnp.where(low, k, v_turned)
                qq = jnp.where(low_half, q[:half], q_turned[half:])
            out_ref[dest, :rows, :] = kv
            out_ref[dest, rows:, :] = qq
    listed = list_ref[...]
    lane = lane_of((listed.shape[0], LANES)) - hd
    allowed = jnp.zeros((listed.shape[0], LANES), jnp.bool_)
    for slot in range(listed.shape[1]):
        allowed = allowed | (listed[:, slot : slot + 1] == lane)
    blocks = listed.shape[0] // nb
    all_bias = jnp.where(allowed, 0.0, NEG)
    for head in range(nb):
        bias[head] = all_bias[head * blocks : (head + 1) * blocks]
    me = lax.axis_index("blk")
    for step in range(nb):
        bias_refs[step][...] = bias[lax.rem(me + step, nb)]


def attend_kernel(nb, scale, g_ref, *rest):
    bias_refs, (out_ref, qx, kx, vx, bias) = rest[:nb], rest[nb:]
    chunks, packed, _ = g_ref.shape
    rows = packed * 2 // 3
    half, hd = rows // 2, LANES // 2
    blocks = chunks * rows // BLOCK
    here = blocks // nb
    me = lax.axis_index("blk")
    for step in range(nb):
        bias[lax.rem(me + nb - step, nb)] = bias_refs[step][...]
    lane = lane_of((rows, LANES))
    low = lane < hd
    low_half = lane_of((half, LANES)) < hd
    one = jnp.ones((rows, LANES), jnp.bfloat16)
    for t in range(chunks):
        b = t * rows // BLOCK
        kv = g_ref[t, :rows, :]
        q = g_ref[t, rows:, :]
        row = jnp.broadcast_to(bias[b // here, b % here : b % here + 1, :], (half, LANES))
        row = row.astype(jnp.bfloat16)
        at = t * rows
        kx[at : at + rows, :] = jnp.where(low, kv, (lane == hd + b).astype(jnp.bfloat16))
        vx[at : at + rows, :] = jnp.where(low, one, kv)
        qx[at : at + half, :] = jnp.where(low_half, q, row)
        qx[at + half : at + rows, :] = jnp.where(low_half, pltpu.roll(q, hd, 1), row)
    group = QGROUP * BLOCK
    later = lax.broadcasted_iota(jnp.int32, (group, group), 1) > lax.broadcasted_iota(
        jnp.int32, (group, group), 0
    )
    factor = scale * math.log2(math.e)
    for g in range(blocks // QGROUP):
        at = g * group
        query = qx[at : at + group, :]
        scores = []
        for c in range(g + 1):
            s = lax.dot_general(
                query,
                kx[c * group : (c + 1) * group, :],
                (((1,), (1,)), ((), ())),
                preferred_element_type=jnp.float32,
            )
            scores.append(jnp.where(later, NEG, s) if c == g else s)
        top = functools.reduce(jnp.maximum, scores)
        top = jnp.max(top, axis=1, keepdims=True)
        total = jnp.zeros((group, LANES), jnp.float32)
        for c in range(g + 1):
            weight = jnp.exp2((scores[c] - top) * factor).astype(jnp.bfloat16)
            total += jnp.dot(
                weight, vx[c * group : (c + 1) * group, :], preferred_element_type=jnp.float32
            )
        turned = pltpu.roll(total, hd, 1)
        for i in range(group // rows):
            a, m, e = i * rows, i * rows + half, (i + 1) * rows
            upper = jnp.where(low_half, turned[a:m], total[m:e])
            lower = jnp.where(low_half, total[a:m], turned[m:e])
            out_ref[at // rows + i] = (upper / lower).astype(jnp.bfloat16)


def unpack_kernel(nu, nb, g_ref, out_ref):
    half, hd = g_ref.shape[1], LANES // 2
    low = lane_of((half, LANES)) < hd
    for pair in range(out_ref.shape[1] // LANES):
        cols = slice(pair * LANES, (pair + 1) * LANES)
        even, odd = 2 * pair, 2 * pair + 1
        a = g_ref[(even % nb) * nu + even // nb]
        b = g_ref[(odd % nb) * nu + odd // nb]
        out_ref[:half, cols] = jnp.where(low, a, pltpu.roll(b, hd, 1))
        out_ref[half:, cols] = jnp.where(low, pltpu.roll(a, hd, 1), b)


def in_vmem(x):
    return pltpu.with_memory_space_constraint(x, pltpu.VMEM)


def by_head(queries, keys, values, block_list):
    nu, nb = lax.axis_size("uly"), lax.axis_size("blk")
    count = nu * nb
    rows, width = queries.shape
    heads_local, here, slots = block_list.shape
    head_dim = width // (heads_local * nu)
    blocks = here * nb
    vmem = pl.BlockSpec(memory_space=pltpu.VMEM)
    small = pltpu.VMEM((here, LANES), jnp.float32)
    packed, *bias = pl.pallas_call(
        functools.partial(pack_kernel, nu, nb),
        out_shape=(pltpu.VMEM((count, rows * 3 // 2, LANES), jnp.bfloat16),) + (small,) * nb,
        in_specs=[vmem] * 4,
        out_specs=(vmem,) * (nb + 1),
        scratch_shapes=[pltpu.VMEM((nb, here, LANES), jnp.float32)],
        cost_estimate=pl.CostEstimate(
            flops=4 * rows * width, bytes_accessed=12 * rows * width, transcendentals=0
        ),
    )(queries, keys, values, block_list.reshape(heads_local * here, slots))
    whole = lax.all_to_all(packed, EVERY, split_axis=0, concat_axis=0)
    moved = [bias[0]] + [
        lax.ppermute(bias[step], "blk", [(i, (i + step) % nb) for i in range(nb)])
        for step in range(1, nb)
    ]
    tokens = count * rows
    attended = pl.pallas_call(
        functools.partial(attend_kernel, nb, head_dim**-0.5),
        out_shape=pltpu.VMEM((count, rows // 2, LANES), jnp.bfloat16),
        in_specs=[vmem] * (nb + 1),
        out_specs=vmem,
        scratch_shapes=[pltpu.VMEM((tokens, LANES), jnp.bfloat16)] * 3
        + [pltpu.VMEM((nb, here, LANES), jnp.float32)],
        cost_estimate=pl.CostEstimate(
            flops=4 * tokens * tokens // 2 * LANES,
            bytes_accessed=4 * tokens * LANES * 2,
            transcendentals=tokens * tokens // 2,
        ),
    )(*(in_vmem(x) for x in (whole, *moved)))
    back = lax.all_to_all(attended, EVERY, split_axis=0, concat_axis=0)
    return pl.pallas_call(
        functools.partial(unpack_kernel, nu, nb),
        out_shape=jax.ShapeDtypeStruct((rows, width), jnp.bfloat16),
        in_specs=[vmem],
        out_specs=vmem,
        cost_estimate=pl.CostEstimate(
            flops=2 * rows * width, bytes_accessed=4 * rows * width, transcendentals=0
        ),
    )(in_vmem(back))


def local(queries, keys, values, block_list):
    nu, nb = lax.axis_size("uly"), lax.axis_size("blk")
    rows, width = queries.shape
    heads_local, here, _ = block_list.shape
    head_dim = width // (heads_local * nu)
    blocks = here * nb
    one_head = (
        heads_local == nb
        and 2 * head_dim == LANES
        and blocks <= LANES // 2
        and blocks % QGROUP == 0
        and BLOCK % rows == 0
        and rows % 32 == 0
    )
    return (by_head if one_head else by_context)(queries, keys, values, block_list)


def solution(mesh):
    placed = (
        P(("blk", "uly"), None),
        P(("blk", "uly"), None),
        P(("blk", "uly"), None),
        P("uly", "blk", None),
    )
    return jax.shard_map(
        local, mesh=mesh, in_specs=placed, out_specs=P(("blk", "uly"), None), check_vma=False
    )
```

```python
import functools
import math

import jax
import jax.numpy as jnp
from jax import lax
from jax.experimental import pallas as pl
from jax.experimental.pallas import tpu as pltpu
from jax.sharding import PartitionSpec as P

BLOCK = 128
QGROUP = 2
LANES = 128
NEG = -1e30
ONES = 16
PIECES = 4
EVERY = ("blk", "uly")


def head_major(token_rows, heads_local, head_dim):
    return token_rows.reshape(token_rows.shape[0] // BLOCK, BLOCK, heads_local, head_dim).transpose(
        2, 0, 1, 3
    )


def select_blocks(source, chosen):
    return jnp.take(source, chosen, axis=0)


def attend_block(operand):
    query_group, key_slots, value_slots, chosen, query_block = operand
    scale = query_group.shape[-1] ** (-0.5)
    scores = (
        jnp.einsum("abd,asjd->absj", query_group, key_slots, preferred_element_type=jnp.float32)
        * scale
    )
    positions = jnp.arange(BLOCK, dtype=jnp.int32)
    query_pos = query_block[:, None] * BLOCK + positions[None, :]
    key_pos = jnp.maximum(chosen, 0)[:, :, None] * BLOCK + positions[None, None, :]
    allowed = (chosen[:, None, :, None] >= 0) & (
        key_pos[:, None, :, :] <= query_pos[:, :, None, None]
    )
    scores = jnp.where(allowed, scores, -1e30)
    row_max = jnp.max(scores, axis=(2, 3), keepdims=True)
    weights = jnp.where(allowed, jnp.exp(scores - row_max), 0.0)
    denominator = jnp.sum(weights, axis=(2, 3))
    rounded = weights.astype(jnp.bfloat16)
    summed = jnp.einsum("absj,asjd->abd", rounded, value_slots, preferred_element_type=jnp.float32)
    return (summed / denominator[:, :, None]).astype(jnp.bfloat16)


def by_context(queries, keys, values, block_list):
    heads_local = block_list.shape[0]
    blocks_dev = block_list.shape[1]
    slot_count = block_list.shape[2]
    head_dim = queries.shape[1] // (heads_local * lax.axis_size("uly"))
    first_block = lax.axis_index("blk") * blocks_dev
    query_rows, key_rows, value_rows = (
        lax.all_to_all(queries, "uly", split_axis=1, concat_axis=0, tiled=True),
        lax.all_to_all(keys, "uly", split_axis=1, concat_axis=0, tiled=True),
        lax.all_to_all(values, "uly", split_axis=1, concat_axis=0, tiled=True),
    )
    keys_all = lax.all_gather(key_rows, "blk", axis=0, tiled=True)
    values_all = lax.all_gather(value_rows, "blk", axis=0, tiled=True)
    chosen = jnp.maximum(block_list, 0)
    key_slots = jax.vmap(select_blocks)(head_major(keys_all, heads_local, head_dim), chosen)
    value_slots = jax.vmap(select_blocks)(head_major(values_all, heads_local, head_dim), chosen)
    groups = heads_local * blocks_dev // QGROUP
    query_heads = head_major(query_rows, heads_local, head_dim).reshape(
        groups, QGROUP, BLOCK, head_dim
    )
    key_groups = key_slots.reshape(groups, QGROUP, slot_count, BLOCK, head_dim)
    value_groups = value_slots.reshape(groups, QGROUP, slot_count, BLOCK, head_dim)
    list_groups = block_list.reshape(groups, QGROUP, slot_count)
    block_numbers = first_block + jnp.arange(blocks_dev, dtype=jnp.int32)
    block_groups = jnp.broadcast_to(block_numbers[None, :], (heads_local, blocks_dev)).reshape(
        groups, QGROUP
    )
    result = lax.map(
        attend_block, (query_heads, key_groups, value_groups, list_groups, block_groups)
    )
    result = result.reshape(heads_local, blocks_dev * BLOCK, head_dim).transpose(1, 0, 2)
    result = result.reshape(blocks_dev * BLOCK, heads_local * head_dim)
    return lax.all_to_all(result, "uly", split_axis=0, concat_axis=1, tiled=True)


def lane_of(shape):
    return lax.broadcasted_iota(jnp.int32, shape, len(shape) - 1)


def pack_kernel(
    nu, nb, q_hbm, k_hbm, v_hbm, list_hbm, out_hbm, *rest
):
    bias_refs, (qkv, listed, packed, bias, in_sems, out_sems, list_sem) = rest[:nb], rest[nb:]
    rows, width = q_hbm.shape
    half, hd = rows // 2, LANES // 2
    pieces = in_sems.shape[0]
    wide, owners = width // pieces, nu // pieces
    low = lane_of((rows, LANES)) < hd
    low_half = lane_of((half, LANES)) < hd
    reads, writes = [], []
    for piece in range(pieces):
        cols = pl.ds(piece * wide, wide)
        reads.append(
            [
                pltpu.make_async_copy(
                    ref.at[:, cols], qkv.at[at, :, cols], in_sems.at[piece, at]
                )
                for at, ref in enumerate((q_hbm, k_hbm, v_hbm))
            ]
        )
        for copy in reads[-1]:
            copy.start()
    list_read = pltpu.make_async_copy(list_hbm, listed, list_sem)
    list_read.start()
    for piece in range(pieces):
        for copy in reads[piece]:
            copy.wait()
        for pair in range(piece * wide // LANES, (piece + 1) * wide // LANES):
            cols = slice(pair * LANES, (pair + 1) * LANES)
            q, k, v = qkv[0, :, cols], qkv[1, :, cols], qkv[2, :, cols]
            k_turned, v_turned = pltpu.roll(k, hd, 1), pltpu.roll(v, hd, 1)
            q_turned = pltpu.roll(q, hd, 1)
            for odd in range(2):
                head = 2 * pair + odd
                if odd:
                    kv = jnp.where(low, k_turned, v)
                    qq = jnp.where(low_half, q_turned[:half], q[half:])
                else:
                    kv = jnp.where(low, k, v_turned)
                    qq = jnp.where(low_half, q[:half], q_turned[half:])
                packed[head % nb, head // nb, :rows, :] = kv
                packed[head % nb, head // nb, rows:, :] = qq
        some = pl.ds(piece * owners, owners)
        writes.append(
            pltpu.make_async_copy(packed.at[:, some], out_hbm.at[:, some], out_sems.at[piece])
        )
        writes[-1].start()
    list_read.wait()
    slots = listed[...]
    lane = lane_of((slots.shape[0], LANES)) - hd
    allowed = jnp.zeros((slots.shape[0], LANES), jnp.bool_)
    for slot in range(slots.shape[1]):
        allowed = allowed | (slots[:, slot : slot + 1] == lane)
    blocks = slots.shape[0] // nb
    all_bias = jnp.where(allowed, 0.0, NEG)
    for head in range(nb):
        bias[head] = all_bias[head * blocks : (head + 1) * blocks]
    me = lax.axis_index("blk")
    for step in range(nb):
        bias_refs[step][...] = bias[lax.rem(me + step, nb)]
    for copy in writes:
        copy.wait()


def attend_kernel(nb, scale, g_ref, *rest):
    bias_refs, (out_ref, qx, kx, vt, st, pt, bias) = rest[:nb], rest[nb:]
    chunks, packed, _ = g_ref.shape
    rows = packed * 2 // 3
    half, hd = rows // 2, LANES // 2
    blocks = chunks * rows // BLOCK
    here = blocks // nb
    me = lax.axis_index("blk")
    for step in range(nb):
        bias[lax.rem(me + nb - step, nb)] = bias_refs[step][...]
    lane = lane_of((rows, LANES))
    low = lane < hd
    low_half = lane_of((half, LANES)) < hd
    group = QGROUP * BLOCK
    each = group // rows
    mid = group // 2
    ones = vt.shape[0] - hd
    vt[:ones, :] = jnp.ones((ones, vt.shape[1]), jnp.bfloat16)
    def prepare(g):
        for t in range(g * each, (g + 1) * each):
            b = t * rows // BLOCK
            kv = g_ref[t, :rows, :]
            q = g_ref[t, rows:, :]
            row = jnp.broadcast_to(bias[b // here, b % here : b % here + 1, :], (half, LANES))
            row = row.astype(jnp.bfloat16)
            kx[t * rows : (t + 1) * rows, :] = jnp.where(low, kv, (lane == hd + b).astype(jnp.bfloat16))
            at = t // each * group + t % each * half
            qx[at : at + half, :] = jnp.where(low_half, q, row)
            qx[at + mid : at + mid + half, :] = jnp.where(low_half, pltpu.roll(q, hd, 1), row)
        for b in range(g * QGROUP, (g + 1) * QGROUP):
            pair = jnp.concatenate([g_ref[b * BLOCK // rows + i, :rows, :] for i in range(BLOCK // rows)], axis=0)
            vt[ones:, b * BLOCK : (b + 1) * BLOCK] = pair.T[hd:, :]
    key = lax.broadcasted_iota(jnp.int32, (group, group), 0)
    col = lax.broadcasted_iota(jnp.int32, (group, group), 1)
    token = col % mid // half * rows + col // mid * half + col % half
    later = key > token
    factor = scale * math.log2(math.e)
    def score(slot, g, c, top):
        s = lax.dot_general(
            kx[c * group : (c + 1) * group, :],
            qx[g * group : (g + 1) * group, :],
            (((1,), (1,)), ((), ())),
            preferred_element_type=jnp.float32,
        )
        if c == g:
            s = jnp.where(later, NEG, s)
        st[slot, c * group : (c + 1) * group, :] = s
        m = jnp.max(s.reshape(group // 8, 8, group), axis=0)
        return m if top is None else jnp.maximum(top, m)
    def weigh(slot, c, top):
        s = st[slot, c * group : (c + 1) * group, :]
        pt[slot, c * group : (c + 1) * group, :] = jnp.exp2((s - top) * factor).astype(jnp.bfloat16)
    def finish(slot, g):
        n = (g + 1) * group
        total = jnp.dot(vt[:, :n], pt[slot, :n, :], preferred_element_type=jnp.float32)
        result = total[ones:] / total[:1]
        pair = jnp.concatenate([result[:, :mid], result[:, mid:]], axis=0)
        out_ref[g * each : (g + 1) * each] = pair.T.astype(jnp.bfloat16).reshape(each, half, LANES)
    ready = set()
    def need(g):
        for i in range(g + 1):
            if i not in ready:
                ready.add(i); prepare(i)
    n = blocks // QGROUP
    order = list(range(n))
    prev = None
    for i, g in enumerate(list(order) + [None]):
        slot = i % 2
        a = [] if g is None else list(range(g + 1))
        b = [] if prev is None else list(range(prev[0] + 1))
        if g is not None: need(g)
        top = None
        for j in range(max(len(a), len(b))):
            if j < len(a): top = score(slot, g, a[j], top)
            if j < len(b): weigh(1 - slot, b[j], prev[1])
        if prev is not None: finish(1 - slot, prev[0])
        if g is not None:
            prev = (g, jnp.max(top, axis=0, keepdims=True))


def unpack_kernel(nu, nb, g_ref, out_ref):
    half, hd = g_ref.shape[1], LANES // 2
    low = lane_of((half, LANES)) < hd
    for pair in range(out_ref.shape[1] // LANES):
        cols = slice(pair * LANES, (pair + 1) * LANES)
        even, odd = 2 * pair, 2 * pair + 1
        a = g_ref[(even % nb) * nu + even // nb]
        b = g_ref[(odd % nb) * nu + odd // nb]
        out_ref[:half, cols] = jnp.where(low, a, pltpu.roll(b, hd, 1))
        out_ref[half:, cols] = jnp.where(low, pltpu.roll(a, hd, 1), b)


def in_vmem(x):
    return pltpu.with_memory_space_constraint(x, pltpu.VMEM)


def by_head(queries, keys, values, block_list):
    nu, nb = lax.axis_size("uly"), lax.axis_size("blk")
    count = nu * nb
    rows, width = queries.shape
    heads_local, here, slots = block_list.shape
    head_dim = width // (heads_local * nu)
    blocks = here * nb
    vmem = pl.BlockSpec(memory_space=pltpu.VMEM)
    small = pltpu.VMEM((here, LANES), jnp.float32)
    anywhere = pl.BlockSpec(memory_space=pl.ANY)
    pieces = math.gcd(nu, PIECES)
    packed, *bias = pl.pallas_call(
        functools.partial(pack_kernel, nu, nb),
        out_shape=(jax.ShapeDtypeStruct((nb, nu, rows * 3 // 2, LANES), jnp.bfloat16),)
        + (small,) * nb,
        in_specs=[anywhere] * 4,
        out_specs=(anywhere,) + (vmem,) * nb,
        scratch_shapes=[
            pltpu.VMEM((3, rows, width), jnp.bfloat16),
            pltpu.VMEM((heads_local * here, slots), jnp.int32),
            pltpu.VMEM((nb, nu, rows * 3 // 2, LANES), jnp.bfloat16),
            pltpu.VMEM((nb, here, LANES), jnp.float32),
            pltpu.SemaphoreType.DMA((pieces, 3)),
            pltpu.SemaphoreType.DMA((pieces,)),
            pltpu.SemaphoreType.DMA,
        ],
        cost_estimate=pl.CostEstimate(
            flops=4 * rows * width, bytes_accessed=12 * rows * width, transcendentals=0
        ),
    )(queries, keys, values, block_list.reshape(heads_local * here, slots))
    packed = packed.reshape(count, rows * 3 // 2, LANES)
    whole = lax.all_to_all(packed, EVERY, split_axis=0, concat_axis=0)
    moved = [bias[0]] + [
        lax.ppermute(bias[step], "blk", [(i, (i + step) % nb) for i in range(nb)])
        for step in range(1, nb)
    ]
    tokens = count * rows
    attended = pl.pallas_call(
        functools.partial(attend_kernel, nb, head_dim**-0.5),
        out_shape=pltpu.VMEM((count, rows // 2, LANES), jnp.bfloat16),
        in_specs=[vmem] * (nb + 1),
        out_specs=vmem,
        scratch_shapes=[
            pltpu.VMEM((tokens, LANES), jnp.bfloat16),
            pltpu.VMEM((tokens, LANES), jnp.bfloat16),
            pltpu.VMEM((head_dim + ONES, tokens), jnp.bfloat16),
            pltpu.VMEM((2, tokens, QGROUP * BLOCK), jnp.float32),
            pltpu.VMEM((2, tokens, QGROUP * BLOCK), jnp.bfloat16),
            pltpu.VMEM((nb, here, LANES), jnp.float32),
        ],
        cost_estimate=pl.CostEstimate(
            flops=4 * tokens * tokens // 2 * LANES,
            bytes_accessed=4 * tokens * LANES * 2,
            transcendentals=tokens * tokens // 2,
        ),
    )(*(in_vmem(x) for x in (whole, *moved)))
    back = lax.all_to_all(attended, EVERY, split_axis=0, concat_axis=0)
    return pl.pallas_call(
        functools.partial(unpack_kernel, nu, nb),
        out_shape=jax.ShapeDtypeStruct((rows, width), jnp.bfloat16),
        in_specs=[vmem],
        out_specs=vmem,
        cost_estimate=pl.CostEstimate(
            flops=2 * rows * width, bytes_accessed=4 * rows * width, transcendentals=0
        ),
    )(in_vmem(back))


def local(queries, keys, values, block_list):
    nu, nb = lax.axis_size("uly"), lax.axis_size("blk")
    rows, width = queries.shape
    heads_local, here, _ = block_list.shape
    head_dim = width // (heads_local * nu)
    blocks = here * nb
    one_head = (
        heads_local == nb
        and 2 * head_dim == LANES
        and blocks <= LANES // 2
        and blocks % QGROUP == 0
        and BLOCK % rows == 0
        and rows % 32 == 0
    )
    return (by_head if one_head else by_context)(queries, keys, values, block_list)


def solution(mesh):
    placed = (
        P(("blk", "uly"), None),
        P(("blk", "uly"), None),
        P(("blk", "uly"), None),
        P("uly", "blk", None),
    )
    return jax.shard_map(
        local, mesh=mesh, in_specs=placed, out_specs=P(("blk", "uly"), None), check_vma=False
    )
```

```python
import functools
import math

import jax
import jax.numpy as jnp
from jax import lax
from jax.experimental import pallas as pl
from jax.experimental.pallas import tpu as pltpu
from jax.sharding import PartitionSpec as P

BLOCK = 128
QGROUP = 2
LANES = 128
NEG = -1e30
ONES = 16
AHEAD = 2
PIECES = 4
EVERY = ("blk", "uly")


def head_major(token_rows, heads_local, head_dim):
    return token_rows.reshape(token_rows.shape[0] // BLOCK, BLOCK, heads_local, head_dim).transpose(
        2, 0, 1, 3
    )


def select_blocks(source, chosen):
    return jnp.take(source, chosen, axis=0)


def attend_block(operand):
    query_group, key_slots, value_slots, chosen, query_block = operand
    scale = query_group.shape[-1] ** (-0.5)
    scores = (
        jnp.einsum("abd,asjd->absj", query_group, key_slots, preferred_element_type=jnp.float32)
        * scale
    )
    positions = jnp.arange(BLOCK, dtype=jnp.int32)
    query_pos = query_block[:, None] * BLOCK + positions[None, :]
    key_pos = jnp.maximum(chosen, 0)[:, :, None] * BLOCK + positions[None, None, :]
    allowed = (chosen[:, None, :, None] >= 0) & (
        key_pos[:, None, :, :] <= query_pos[:, :, None, None]
    )
    scores = jnp.where(allowed, scores, -1e30)
    row_max = jnp.max(scores, axis=(2, 3), keepdims=True)
    weights = jnp.where(allowed, jnp.exp(scores - row_max), 0.0)
    denominator = jnp.sum(weights, axis=(2, 3))
    rounded = weights.astype(jnp.bfloat16)
    summed = jnp.einsum("absj,asjd->abd", rounded, value_slots, preferred_element_type=jnp.float32)
    return (summed / denominator[:, :, None]).astype(jnp.bfloat16)


def by_context(queries, keys, values, block_list):
    heads_local = block_list.shape[0]
    blocks_dev = block_list.shape[1]
    slot_count = block_list.shape[2]
    head_dim = queries.shape[1] // (heads_local * lax.axis_size("uly"))
    first_block = lax.axis_index("blk") * blocks_dev
    query_rows, key_rows, value_rows = (
        lax.all_to_all(queries, "uly", split_axis=1, concat_axis=0, tiled=True),
        lax.all_to_all(keys, "uly", split_axis=1, concat_axis=0, tiled=True),
        lax.all_to_all(values, "uly", split_axis=1, concat_axis=0, tiled=True),
    )
    keys_all = lax.all_gather(key_rows, "blk", axis=0, tiled=True)
    values_all = lax.all_gather(value_rows, "blk", axis=0, tiled=True)
    chosen = jnp.maximum(block_list, 0)
    key_slots = jax.vmap(select_blocks)(head_major(keys_all, heads_local, head_dim), chosen)
    value_slots = jax.vmap(select_blocks)(head_major(values_all, heads_local, head_dim), chosen)
    groups = heads_local * blocks_dev // QGROUP
    query_heads = head_major(query_rows, heads_local, head_dim).reshape(
        groups, QGROUP, BLOCK, head_dim
    )
    key_groups = key_slots.reshape(groups, QGROUP, slot_count, BLOCK, head_dim)
    value_groups = value_slots.reshape(groups, QGROUP, slot_count, BLOCK, head_dim)
    list_groups = block_list.reshape(groups, QGROUP, slot_count)
    block_numbers = first_block + jnp.arange(blocks_dev, dtype=jnp.int32)
    block_groups = jnp.broadcast_to(block_numbers[None, :], (heads_local, blocks_dev)).reshape(
        groups, QGROUP
    )
    result = lax.map(
        attend_block, (query_heads, key_groups, value_groups, list_groups, block_groups)
    )
    result = result.reshape(heads_local, blocks_dev * BLOCK, head_dim).transpose(1, 0, 2)
    result = result.reshape(blocks_dev * BLOCK, heads_local * head_dim)
    return lax.all_to_all(result, "uly", split_axis=0, concat_axis=1, tiled=True)


def lane_of(shape):
    return lax.broadcasted_iota(jnp.int32, shape, len(shape) - 1)


def pack_kernel(
    nu, nb, q_hbm, k_hbm, v_hbm, list_hbm, out_hbm, *rest
):
    bias_refs, (qkv, listed, packed, bias, in_sems, out_sems, list_sem) = rest[:nb], rest[nb:]
    rows, width = q_hbm.shape
    half, hd = rows // 2, LANES // 2
    pieces = in_sems.shape[0]
    wide, owners = width // pieces, nu // pieces
    low = lane_of((rows, LANES)) < hd
    low_half = lane_of((half, LANES)) < hd
    reads, writes = [], []
    for piece in range(pieces):
        cols = pl.ds(piece * wide, wide)
        reads.append(
            [
                pltpu.make_async_copy(
                    ref.at[:, cols], qkv.at[at, :, cols], in_sems.at[piece, at]
                )
                for at, ref in enumerate((q_hbm, k_hbm, v_hbm))
            ]
        )
        for copy in reads[-1]:
            copy.start()
    list_read = pltpu.make_async_copy(list_hbm, listed, list_sem)
    list_read.start()
    for piece in range(pieces):
        for copy in reads[piece]:
            copy.wait()
        for pair in range(piece * wide // LANES, (piece + 1) * wide // LANES):
            cols = slice(pair * LANES, (pair + 1) * LANES)
            q, k, v = qkv[0, :, cols], qkv[1, :, cols], qkv[2, :, cols]
            k_turned, v_turned = pltpu.roll(k, hd, 1), pltpu.roll(v, hd, 1)
            q_turned = pltpu.roll(q, hd, 1)
            for odd in range(2):
                head = 2 * pair + odd
                if odd:
                    kv = jnp.where(low, k_turned, v)
                    qq = jnp.where(low_half, q_turned[:half], q[half:])
                else:
                    kv = jnp.where(low, k, v_turned)
                    qq = jnp.where(low_half, q[:half], q_turned[half:])
                packed[head % nb, head // nb, :rows, :] = kv
                packed[head % nb, head // nb, rows:, :] = qq
        some = pl.ds(piece * owners, owners)
        writes.append(
            pltpu.make_async_copy(packed.at[:, some], out_hbm.at[:, some], out_sems.at[piece])
        )
        writes[-1].start()
    list_read.wait()
    slots = listed[...]
    lane = lane_of((slots.shape[0], LANES)) - hd
    allowed = jnp.zeros((slots.shape[0], LANES), jnp.bool_)
    for slot in range(slots.shape[1]):
        allowed = allowed | (slots[:, slot : slot + 1] == lane)
    blocks = slots.shape[0] // nb
    all_bias = jnp.where(allowed, 0.0, NEG)
    for head in range(nb):
        bias[head] = all_bias[head * blocks : (head + 1) * blocks]
    me = lax.axis_index("blk")
    for step in range(nb):
        bias_refs[step][...] = bias[lax.rem(me + step, nb)]
    for copy in writes:
        copy.wait()


def attend_kernel(nb, scale, g_ref, *rest):
    bias_refs, (out_ref, qx, kx, vt, st, pt, bias) = rest[:nb], rest[nb:]
    chunks, packed, _ = g_ref.shape
    rows = packed * 2 // 3
    half, hd = rows // 2, LANES // 2
    blocks = chunks * rows // BLOCK
    here = blocks // nb
    me = lax.axis_index("blk")
    for step in range(nb):
        bias[lax.rem(me + nb - step, nb)] = bias_refs[step][...]
    lane = lane_of((rows, LANES))
    low = lane < hd
    low_half = lane_of((half, LANES)) < hd
    group = QGROUP * BLOCK
    each = group // rows
    mid = group // 2
    ones = vt.shape[0] - hd
    vt[:ones, :] = jnp.ones((ones, vt.shape[1]), jnp.bfloat16)
    def prepare(g):
        for t in range(g * each, (g + 1) * each):
            b = t * rows // BLOCK
            kv = g_ref[t, :rows, :]
            q = g_ref[t, rows:, :]
            row = jnp.broadcast_to(bias[b // here, b % here : b % here + 1, :], (half, LANES))
            row = row.astype(jnp.bfloat16)
            kx[t * rows : (t + 1) * rows, :] = jnp.where(low, kv, (lane == hd + b).astype(jnp.bfloat16))
            at = t // each * group + t % each * half
            qx[at : at + half, :] = jnp.where(low_half, q, row)
            qx[at + mid : at + mid + half, :] = jnp.where(low_half, pltpu.roll(q, hd, 1), row)
        for b in range(g * QGROUP, (g + 1) * QGROUP):
            pair = jnp.concatenate([g_ref[b * BLOCK // rows + i, :rows, :] for i in range(BLOCK // rows)], axis=0)
            vt[ones:, b * BLOCK : (b + 1) * BLOCK] = pair.T[hd:, :]
    key = lax.broadcasted_iota(jnp.int32, (group, group), 0)
    col = lax.broadcasted_iota(jnp.int32, (group, group), 1)
    token = col % mid // half * rows + col // mid * half + col % half
    later = key > token
    factor = scale * math.log2(math.e)
    def score(slot, g, c, top):
        s = lax.dot_general(
            kx[c * group : (c + 1) * group, :],
            qx[g * group : (g + 1) * group, :],
            (((1,), (1,)), ((), ())),
            preferred_element_type=jnp.float32,
        )
        if c == g:
            s = jnp.where(later, NEG, s)
        st[slot, c * group : (c + 1) * group, :] = s
        m = jnp.max(s.reshape(group // 8, 8, group), axis=0)
        return m if top is None else jnp.maximum(top, m)
    def weigh(slot, c, top):
        s = st[slot, c * group : (c + 1) * group, :]
        pt[slot, c * group : (c + 1) * group, :] = jnp.exp2((s - top) * factor).astype(jnp.bfloat16)
    def gather(slot, c0, c1, total):
        part = jnp.dot(
            vt[:, c0 * group : c1 * group], pt[slot, c0 * group : c1 * group, :],
            preferred_element_type=jnp.float32,
        )
        return part if total is None else total + part
    def finish(g, total):
        result = total[ones:] / total[:1]
        pair = jnp.concatenate([result[:, :mid], result[:, mid:]], axis=0)
        out_ref[g * each : (g + 1) * each] = pair.T.astype(jnp.bfloat16).reshape(each, half, LANES)
    ready = set()
    def need(g):
        for i in range(g + 1):
            if i not in ready:
                ready.add(i); prepare(i)
    n = blocks // QGROUP
    order = list(range(1, n, 2)) + list(range(0, n, 2))[::-1]
    tops, slots = {}, AHEAD + 1
    for i in range(n + AHEAD):
        g = order[i] if i < n else None
        w = order[i - AHEAD] if i >= AHEAD else None
        a = [] if g is None else list(range(g + 1))
        b = [] if w is None else list(range(w + 1))
        if g is not None: need(g)
        top, total, done = None, None, 0
        k = 0
        for j in range(max(len(a), len(b))):
            while k < len(b) and (not a or k * len(a) <= j * len(b)):
                weigh((i - AHEAD) % slots, b[k], tops[w])
                k += 1
            if j < len(a): top = score(i % slots, g, a[j], top)
        while k < len(b):
            weigh((i - AHEAD) % slots, b[k], tops[w]); k += 1
        if g is not None:
            tops[g] = jnp.max(top, axis=0, keepdims=True)
        if w is not None:
            finish(w, gather((i - AHEAD) % slots, 0, w + 1, None))


def unpack_kernel(nu, nb, g_ref, out_ref):
    half, hd = g_ref.shape[1], LANES // 2
    low = lane_of((half, LANES)) < hd
    for pair in range(out_ref.shape[1] // LANES):
        cols = slice(pair * LANES, (pair + 1) * LANES)
        even, odd = 2 * pair, 2 * pair + 1
        a = g_ref[(even % nb) * nu + even // nb]
        b = g_ref[(odd % nb) * nu + odd // nb]
        out_ref[:half, cols] = jnp.where(low, a, pltpu.roll(b, hd, 1))
        out_ref[half:, cols] = jnp.where(low, pltpu.roll(a, hd, 1), b)


def in_vmem(x):
    return pltpu.with_memory_space_constraint(x, pltpu.VMEM)


def by_head(queries, keys, values, block_list):
    nu, nb = lax.axis_size("uly"), lax.axis_size("blk")
    count = nu * nb
    rows, width = queries.shape
    heads_local, here, slots = block_list.shape
    head_dim = width // (heads_local * nu)
    blocks = here * nb
    vmem = pl.BlockSpec(memory_space=pltpu.VMEM)
    small = pltpu.VMEM((here, LANES), jnp.float32)
    anywhere = pl.BlockSpec(memory_space=pl.ANY)
    pieces = math.gcd(nu, PIECES)
    packed, *bias = pl.pallas_call(
        functools.partial(pack_kernel, nu, nb),
        out_shape=(jax.ShapeDtypeStruct((nb, nu, rows * 3 // 2, LANES), jnp.bfloat16),)
        + (small,) * nb,
        in_specs=[anywhere] * 4,
        out_specs=(anywhere,) + (vmem,) * nb,
        scratch_shapes=[
            pltpu.VMEM((3, rows, width), jnp.bfloat16),
            pltpu.VMEM((heads_local * here, slots), jnp.int32),
            pltpu.VMEM((nb, nu, rows * 3 // 2, LANES), jnp.bfloat16),
            pltpu.VMEM((nb, here, LANES), jnp.float32),
            pltpu.SemaphoreType.DMA((pieces, 3)),
            pltpu.SemaphoreType.DMA((pieces,)),
            pltpu.SemaphoreType.DMA,
        ],
        cost_estimate=pl.CostEstimate(
            flops=4 * rows * width, bytes_accessed=12 * rows * width, transcendentals=0
        ),
    )(queries, keys, values, block_list.reshape(heads_local * here, slots))
    packed = packed.reshape(count, rows * 3 // 2, LANES)
    whole = lax.all_to_all(packed, EVERY, split_axis=0, concat_axis=0)
    moved = [bias[0]] + [
        lax.ppermute(bias[step], "blk", [(i, (i + step) % nb) for i in range(nb)])
        for step in range(1, nb)
    ]
    tokens = count * rows
    attended = pl.pallas_call(
        functools.partial(attend_kernel, nb, head_dim**-0.5),
        out_shape=pltpu.VMEM((count, rows // 2, LANES), jnp.bfloat16),
        in_specs=[vmem] * (nb + 1),
        out_specs=vmem,
        scratch_shapes=[
            pltpu.VMEM((tokens, LANES), jnp.bfloat16),
            pltpu.VMEM((tokens, LANES), jnp.bfloat16),
            pltpu.VMEM((head_dim + ONES, tokens), jnp.bfloat16),
            pltpu.VMEM((AHEAD + 1, tokens, QGROUP * BLOCK), jnp.float32),
            pltpu.VMEM((AHEAD + 1, tokens, QGROUP * BLOCK), jnp.bfloat16),
            pltpu.VMEM((nb, here, LANES), jnp.float32),
        ],
        cost_estimate=pl.CostEstimate(
            flops=4 * tokens * tokens // 2 * LANES,
            bytes_accessed=4 * tokens * LANES * 2,
            transcendentals=tokens * tokens // 2,
        ),
    )(*(in_vmem(x) for x in (whole, *moved)))
    back = lax.all_to_all(attended, EVERY, split_axis=0, concat_axis=0)
    return pl.pallas_call(
        functools.partial(unpack_kernel, nu, nb),
        out_shape=jax.ShapeDtypeStruct((rows, width), jnp.bfloat16),
        in_specs=[vmem],
        out_specs=vmem,
        cost_estimate=pl.CostEstimate(
            flops=2 * rows * width, bytes_accessed=4 * rows * width, transcendentals=0
        ),
    )(in_vmem(back))


def local(queries, keys, values, block_list):
    nu, nb = lax.axis_size("uly"), lax.axis_size("blk")
    rows, width = queries.shape
    heads_local, here, _ = block_list.shape
    head_dim = width // (heads_local * nu)
    blocks = here * nb
    one_head = (
        heads_local == nb
        and 2 * head_dim == LANES
        and blocks <= LANES // 2
        and blocks % QGROUP == 0
        and BLOCK % rows == 0
        and rows % 32 == 0
    )
    return (by_head if one_head else by_context)(queries, keys, values, block_list)


def solution(mesh):
    placed = (
        P(("blk", "uly"), None),
        P(("blk", "uly"), None),
        P(("blk", "uly"), None),
        P("uly", "blk", None),
    )
    return jax.shard_map(
        local, mesh=mesh, in_specs=placed, out_specs=P(("blk", "uly"), None), check_vma=False
    )
```

```python
import functools
import math

import jax
import jax.numpy as jnp
from jax import lax
from jax.experimental import pallas as pl
from jax.experimental.pallas import tpu as pltpu
from jax.sharding import PartitionSpec as P

BLOCK = 128
QGROUP = 2
LANES = 128
NEG = -1e30
ONES = 16
AHEAD = 2
PIECES = 4
EVERY = ("uly", "blk")


def head_major(token_rows, heads_local, head_dim):
    return token_rows.reshape(token_rows.shape[0] // BLOCK, BLOCK, heads_local, head_dim).transpose(
        2, 0, 1, 3
    )


def select_blocks(source, chosen):
    return jnp.take(source, chosen, axis=0)


def attend_block(operand):
    query_group, key_slots, value_slots, chosen, query_block = operand
    scale = query_group.shape[-1] ** (-0.5)
    scores = (
        jnp.einsum("abd,asjd->absj", query_group, key_slots, preferred_element_type=jnp.float32)
        * scale
    )
    positions = jnp.arange(BLOCK, dtype=jnp.int32)
    query_pos = query_block[:, None] * BLOCK + positions[None, :]
    key_pos = jnp.maximum(chosen, 0)[:, :, None] * BLOCK + positions[None, None, :]
    allowed = (chosen[:, None, :, None] >= 0) & (
        key_pos[:, None, :, :] <= query_pos[:, :, None, None]
    )
    scores = jnp.where(allowed, scores, -1e30)
    row_max = jnp.max(scores, axis=(2, 3), keepdims=True)
    weights = jnp.where(allowed, jnp.exp(scores - row_max), 0.0)
    denominator = jnp.sum(weights, axis=(2, 3))
    rounded = weights.astype(jnp.bfloat16)
    summed = jnp.einsum("absj,asjd->abd", rounded, value_slots, preferred_element_type=jnp.float32)
    return (summed / denominator[:, :, None]).astype(jnp.bfloat16)


def by_context(queries, keys, values, block_list):
    heads_local = block_list.shape[0]
    blocks_dev = block_list.shape[1]
    slot_count = block_list.shape[2]
    head_dim = queries.shape[1] // (heads_local * lax.axis_size("uly"))
    first_block = lax.axis_index("blk") * blocks_dev
    query_rows, key_rows, value_rows = (
        lax.all_to_all(queries, "uly", split_axis=1, concat_axis=0, tiled=True),
        lax.all_to_all(keys, "uly", split_axis=1, concat_axis=0, tiled=True),
        lax.all_to_all(values, "uly", split_axis=1, concat_axis=0, tiled=True),
    )
    keys_all = lax.all_gather(key_rows, "blk", axis=0, tiled=True)
    values_all = lax.all_gather(value_rows, "blk", axis=0, tiled=True)
    chosen = jnp.maximum(block_list, 0)
    key_slots = jax.vmap(select_blocks)(head_major(keys_all, heads_local, head_dim), chosen)
    value_slots = jax.vmap(select_blocks)(head_major(values_all, heads_local, head_dim), chosen)
    groups = heads_local * blocks_dev // QGROUP
    query_heads = head_major(query_rows, heads_local, head_dim).reshape(
        groups, QGROUP, BLOCK, head_dim
    )
    key_groups = key_slots.reshape(groups, QGROUP, slot_count, BLOCK, head_dim)
    value_groups = value_slots.reshape(groups, QGROUP, slot_count, BLOCK, head_dim)
    list_groups = block_list.reshape(groups, QGROUP, slot_count)
    block_numbers = first_block + jnp.arange(blocks_dev, dtype=jnp.int32)
    block_groups = jnp.broadcast_to(block_numbers[None, :], (heads_local, blocks_dev)).reshape(
        groups, QGROUP
    )
    result = lax.map(
        attend_block, (query_heads, key_groups, value_groups, list_groups, block_groups)
    )
    result = result.reshape(heads_local, blocks_dev * BLOCK, head_dim).transpose(1, 0, 2)
    result = result.reshape(blocks_dev * BLOCK, heads_local * head_dim)
    return lax.all_to_all(result, "uly", split_axis=0, concat_axis=1, tiled=True)


def place(device, nu, nb):
    u, b = divmod(device, nb)
    return (u % 2 * (nu // 2) + u // 2) * nb + b


def lane_of(shape):
    return lax.broadcasted_iota(jnp.int32, shape, len(shape) - 1)


def pack_kernel(nb, q_hbm, k_hbm, v_hbm, list_hbm, out_hbm, *rest):
    bias_refs, (qkv, listed, packed, bias, in_sems, out_sems, list_sem) = rest[:nb], rest[nb:]
    rows, width = q_hbm.shape
    half, hd = rows // 2, LANES // 2
    pieces = in_sems.shape[0]
    wide, part = width // pieces, out_hbm.shape[1] // pieces
    low = lane_of((rows, LANES)) < hd
    low_half = lane_of((half, LANES)) < hd
    reads, writes = [], []
    for piece in range(pieces):
        cols = pl.ds(piece * wide, wide)
        reads.append(
            [
                pltpu.make_async_copy(
                    ref.at[:, cols], qkv.at[at, :, cols], in_sems.at[piece, at]
                )
                for at, ref in enumerate((q_hbm, k_hbm, v_hbm))
            ]
        )
        for copy in reads[-1]:
            copy.start()
    list_read = pltpu.make_async_copy(list_hbm, listed, list_sem)
    list_read.start()
    for piece in range(pieces):
        for copy in reads[piece]:
            copy.wait()
        for pair in range(piece * wide // LANES, (piece + 1) * wide // LANES):
            cols = slice(pair * LANES, (pair + 1) * LANES)
            q, k, v = qkv[0, :, cols], qkv[1, :, cols], qkv[2, :, cols]
            k_turned, v_turned = pltpu.roll(k, hd, 1), pltpu.roll(v, hd, 1)
            q_turned = pltpu.roll(q, hd, 1)
            for odd in range(2):
                u, b = divmod(2 * pair + odd, nb)
                if odd:
                    kv = jnp.where(low, k_turned, v)
                    qq = jnp.where(low_half, q_turned[:half], q[half:])
                else:
                    kv = jnp.where(low, k, v_turned)
                    qq = jnp.where(low_half, q[:half], q_turned[half:])
                packed[u % 2, u // 2, b, :rows, :] = kv
                packed[u % 2, u // 2, b, rows:, :] = qq
        some = pl.ds(piece * part, part)
        writes.append(
            pltpu.make_async_copy(packed.at[:, some], out_hbm.at[:, some], out_sems.at[piece])
        )
        writes[-1].start()
    list_read.wait()
    slots = listed[...]
    lane = lane_of((slots.shape[0], LANES)) - hd
    allowed = jnp.zeros((slots.shape[0], LANES), jnp.bool_)
    for slot in range(slots.shape[1]):
        allowed = allowed | (slots[:, slot : slot + 1] == lane)
    blocks = slots.shape[0] // nb
    all_bias = jnp.where(allowed, 0.0, NEG)
    for head in range(nb):
        bias[head] = all_bias[head * blocks : (head + 1) * blocks]
    me = lax.axis_index("blk")
    for step in range(nb):
        bias_refs[step][...] = bias[lax.rem(me + step, nb)]
    for copy in writes:
        copy.wait()


def attend_kernel(nu, nb, scale, g_ref, *rest):
    bias_refs, (out_ref, qx, kx, vt, bias) = rest[:nb], rest[nb:]
    chunks, packed, _ = g_ref.shape
    rows = packed * 2 // 3
    half, hd = rows // 2, LANES // 2
    blocks = chunks * rows // BLOCK
    here = blocks // nb
    me = lax.axis_index("blk")
    for step in range(nb):
        bias[lax.rem(me + nb - step, nb)] = bias_refs[step][...]
    lane = lane_of((rows, LANES))
    low = lane < hd
    low_half = lane_of((half, LANES)) < hd
    group = QGROUP * BLOCK
    each = group // rows
    mid = group // 2
    ones = vt.shape[0] - hd
    vt[:ones, :] = jnp.ones((ones, vt.shape[1]), jnp.bfloat16)

    def owner(t):
        return place(t % nu * nb + t // nu, nu, nb)

    def prepare(g):
        for t in range(g * each, (g + 1) * each):
            b = t * rows // BLOCK
            kv = g_ref[owner(t), :rows, :]
            q = g_ref[owner(t), rows:, :]
            row = jnp.broadcast_to(bias[b // here, b % here : b % here + 1, :], (half, LANES))
            row = row.astype(jnp.bfloat16)
            kx[t * rows : (t + 1) * rows, :] = jnp.where(low, kv, (lane == hd + b).astype(jnp.bfloat16))
            at = t // each * group + t % each * half
            qx[at : at + half, :] = jnp.where(low_half, q, row)
            qx[at + mid : at + mid + half, :] = jnp.where(low_half, pltpu.roll(q, hd, 1), row)
        for b in range(g * QGROUP, (g + 1) * QGROUP):
            pair = jnp.concatenate([g_ref[owner(b * BLOCK // rows + i), :rows, :] for i in range(BLOCK // rows)], axis=0)
            vt[ones:, b * BLOCK : (b + 1) * BLOCK] = pair.T[hd:, :]
    key = lax.broadcasted_iota(jnp.int32, (group, group), 0)
    col = lax.broadcasted_iota(jnp.int32, (group, group), 1)
    token = col % mid // half * rows + col // mid * half + col % half
    later = key > token
    factor = scale * math.log2(math.e)
    held = {}
    def score(slot, g, c, e, top):
        s = lax.dot_general(
            kx[c * group : e * group, :],
            qx[g * group : (g + 1) * group, :],
            (((1,), (1,)), ((), ())),
            preferred_element_type=jnp.float32,
        )
        for t in range(c, e):
            tile = s[(t - c) * group : (t - c + 1) * group]
            if t == g:
                tile = jnp.where(later, NEG, tile)
            held[slot, t] = tile
            m = jnp.max(tile.reshape(group // 8, 8, group), axis=0)
            top = m if top is None else jnp.maximum(top, m)
        return top
    def weigh(slot, c, top):
        s = held[slot, c]
        held[slot, c] = jnp.exp2((s - top) * factor).astype(jnp.bfloat16)
    def gather(slot, c0, c1, total):
        part = jnp.dot(
            vt[:, c0 * group : c1 * group], jnp.concatenate([held[slot, x] for x in range(c0, c1)], axis=0),
            preferred_element_type=jnp.float32,
        )
        return part if total is None else total + part
    def finish(g, total):
        result = (total[ones:].reshape(hd // 8, 8, group) * (1.0 / total[:8])[None]).reshape(hd, group)
        pair = jnp.concatenate([result[:, :mid], result[:, mid:]], axis=0)
        chunk = pair.T.astype(jnp.bfloat16)
        for i in range(each):
            out_ref[owner(g * each + i)] = chunk[i * half : (i + 1) * half]
    ready = set()
    def need(g):
        for i in range(g + 1):
            if i not in ready:
                ready.add(i); prepare(i)
    n = blocks // QGROUP
    order = list(range(1, n, 2)) + list(range(0, n, 2))[::-1]
    tops, slots = {}, AHEAD + 1
    for i in range(n + AHEAD):
        g = order[i] if i < n else None
        w = order[i - AHEAD] if i >= AHEAD else None
        a = [] if g is None else list(range(g + 1))
        b = [] if w is None else list(range(w + 1))
        if g is not None: need(g)
        top, total, done = None, None, 0
        k = 0
        for j in range(max(len(a), len(b))):
            while k < len(b) and (not a or k * len(a) <= j * len(b)):
                weigh((i - AHEAD) % slots, b[k], tops[w])
                k += 1
            if j < len(a) and j % 2 == 0:
                top = score(i % slots, g, j, min(j + 2, len(a)), top)
        while k < len(b):
            weigh((i - AHEAD) % slots, b[k], tops[w]); k += 1
        if g is not None:
            tops[g] = jnp.max(top, axis=0, keepdims=True)
        if w is not None:
            finish(w, gather((i - AHEAD) % slots, 0, w + 1, None))


def unpack_kernel(nu, nb, g_ref, out_ref):
    half, hd = g_ref.shape[1], LANES // 2
    low = lane_of((half, LANES)) < hd
    for pair in range(out_ref.shape[1] // LANES):
        cols = slice(pair * LANES, (pair + 1) * LANES)
        a, b = (g_ref[place(2 * pair + odd, nu, nb)] for odd in range(2))
        out_ref[:half, cols] = jnp.where(low, a, pltpu.roll(b, hd, 1))
        out_ref[half:, cols] = jnp.where(low, pltpu.roll(a, hd, 1), b)


def exchange(chunks, nu, nb):
    order = [u * nb + b for odd in range(2) for u in range(odd, nu, 2) for b in range(nb)]
    return lax.all_to_all(chunks, EVERY, split_axis=0, concat_axis=0, axis_index_groups=[order])


def in_vmem(x):
    return pltpu.with_memory_space_constraint(x, pltpu.VMEM)


def by_head(queries, keys, values, block_list):
    nu, nb = lax.axis_size("uly"), lax.axis_size("blk")
    count = nu * nb
    rows, width = queries.shape
    heads_local, here, slots = block_list.shape
    head_dim = width // (heads_local * nu)
    blocks = here * nb
    vmem = pl.BlockSpec(memory_space=pltpu.VMEM)
    small = pltpu.VMEM((here, LANES), jnp.float32)
    anywhere = pl.BlockSpec(memory_space=pl.ANY)
    pieces = math.gcd(nu // 2, PIECES)
    laid = (2, nu // 2, nb, rows * 3 // 2, LANES)
    packed, *bias = pl.pallas_call(
        functools.partial(pack_kernel, nb),
        out_shape=(jax.ShapeDtypeStruct(laid, jnp.bfloat16),)
        + (small,) * nb,
        in_specs=[anywhere] * 4,
        out_specs=(anywhere,) + (vmem,) * nb,
        scratch_shapes=[
            pltpu.VMEM((3, rows, width), jnp.bfloat16),
            pltpu.VMEM((heads_local * here, slots), jnp.int32),
            pltpu.VMEM(laid, jnp.bfloat16),
            pltpu.VMEM((nb, here, LANES), jnp.float32),
            pltpu.SemaphoreType.DMA((pieces, 3)),
            pltpu.SemaphoreType.DMA((pieces,)),
            pltpu.SemaphoreType.DMA,
        ],
        cost_estimate=pl.CostEstimate(
            flops=4 * rows * width, bytes_accessed=12 * rows * width, transcendentals=0
        ),
    )(queries, keys, values, block_list.reshape(heads_local * here, slots))
    whole = exchange(packed.reshape(count, rows * 3 // 2, LANES), nu, nb)
    moved = [bias[0]] + [
        lax.ppermute(bias[step], "blk", [(i, (i + step) % nb) for i in range(nb)])
        for step in range(1, nb)
    ]
    tokens = count * rows
    attended = pl.pallas_call(
        functools.partial(attend_kernel, nu, nb, head_dim**-0.5),
        out_shape=pltpu.VMEM((count, rows // 2, LANES), jnp.bfloat16),
        in_specs=[vmem] * (nb + 1),
        out_specs=vmem,
        scratch_shapes=[
            pltpu.VMEM((tokens, LANES), jnp.bfloat16),
            pltpu.VMEM((tokens, LANES), jnp.bfloat16),
            pltpu.VMEM((head_dim + ONES, tokens), jnp.bfloat16),
            pltpu.VMEM((nb, here, LANES), jnp.float32),
        ],
        cost_estimate=pl.CostEstimate(
            flops=4 * tokens * tokens // 2 * LANES,
            bytes_accessed=4 * tokens * LANES * 2,
            transcendentals=tokens * tokens // 2,
        ),
    )(*(in_vmem(x) for x in (whole, *moved)))
    back = exchange(attended, nu, nb)
    return pl.pallas_call(
        functools.partial(unpack_kernel, nu, nb),
        out_shape=jax.ShapeDtypeStruct((rows, width), jnp.bfloat16),
        in_specs=[vmem],
        out_specs=vmem,
        cost_estimate=pl.CostEstimate(
            flops=2 * rows * width, bytes_accessed=4 * rows * width, transcendentals=0
        ),
    )(in_vmem(back))


def local(queries, keys, values, block_list):
    nu, nb = lax.axis_size("uly"), lax.axis_size("blk")
    rows, width = queries.shape
    heads_local, here, _ = block_list.shape
    head_dim = width // (heads_local * nu)
    blocks = here * nb
    one_head = (
        heads_local == nb
        and nu % 2 == 0
        and 2 * head_dim == LANES
        and blocks <= LANES // 2
        and blocks % QGROUP == 0
        and BLOCK % rows == 0
        and rows % 32 == 0
    )
    return (by_head if one_head else by_context)(queries, keys, values, block_list)


def solution(mesh):
    placed = (
        P(("blk", "uly"), None),
        P(("blk", "uly"), None),
        P(("blk", "uly"), None),
        P("uly", "blk", None),
    )
    return jax.shard_map(
        local, mesh=mesh, in_specs=placed, out_specs=P(("blk", "uly"), None), check_vma=False
    )
```

```python
import functools
import math

import jax
import jax.numpy as jnp
from jax import lax
from jax.experimental import pallas as pl
from jax.experimental.pallas import tpu as pltpu
from jax.sharding import PartitionSpec as P

BLOCK = 128
QGROUP = 2
LANES = 128
NEG = -1e30
ONES = 16
AHEAD = 2
PIECES = 4
EVERY = ("uly", "blk")


def head_major(token_rows, heads_local, head_dim):
    return token_rows.reshape(token_rows.shape[0] // BLOCK, BLOCK, heads_local, head_dim).transpose(
        2, 0, 1, 3
    )


def select_blocks(source, chosen):
    return jnp.take(source, chosen, axis=0)


def attend_block(operand):
    query_group, key_slots, value_slots, chosen, query_block = operand
    scale = query_group.shape[-1] ** (-0.5)
    scores = (
        jnp.einsum("abd,asjd->absj", query_group, key_slots, preferred_element_type=jnp.float32)
        * scale
    )
    positions = jnp.arange(BLOCK, dtype=jnp.int32)
    query_pos = query_block[:, None] * BLOCK + positions[None, :]
    key_pos = jnp.maximum(chosen, 0)[:, :, None] * BLOCK + positions[None, None, :]
    allowed = (chosen[:, None, :, None] >= 0) & (
        key_pos[:, None, :, :] <= query_pos[:, :, None, None]
    )
    scores = jnp.where(allowed, scores, -1e30)
    row_max = jnp.max(scores, axis=(2, 3), keepdims=True)
    weights = jnp.where(allowed, jnp.exp(scores - row_max), 0.0)
    denominator = jnp.sum(weights, axis=(2, 3))
    rounded = weights.astype(jnp.bfloat16)
    summed = jnp.einsum("absj,asjd->abd", rounded, value_slots, preferred_element_type=jnp.float32)
    return (summed / denominator[:, :, None]).astype(jnp.bfloat16)


def by_context(queries, keys, values, block_list):
    heads_local = block_list.shape[0]
    blocks_dev = block_list.shape[1]
    slot_count = block_list.shape[2]
    head_dim = queries.shape[1] // (heads_local * lax.axis_size("uly"))
    first_block = lax.axis_index("blk") * blocks_dev
    query_rows, key_rows, value_rows = (
        lax.all_to_all(queries, "uly", split_axis=1, concat_axis=0, tiled=True),
        lax.all_to_all(keys, "uly", split_axis=1, concat_axis=0, tiled=True),
        lax.all_to_all(values, "uly", split_axis=1, concat_axis=0, tiled=True),
    )
    keys_all = lax.all_gather(key_rows, "blk", axis=0, tiled=True)
    values_all = lax.all_gather(value_rows, "blk", axis=0, tiled=True)
    chosen = jnp.maximum(block_list, 0)
    key_slots = jax.vmap(select_blocks)(head_major(keys_all, heads_local, head_dim), chosen)
    value_slots = jax.vmap(select_blocks)(head_major(values_all, heads_local, head_dim), chosen)
    groups = heads_local * blocks_dev // QGROUP
    query_heads = head_major(query_rows, heads_local, head_dim).reshape(
        groups, QGROUP, BLOCK, head_dim
    )
    key_groups = key_slots.reshape(groups, QGROUP, slot_count, BLOCK, head_dim)
    value_groups = value_slots.reshape(groups, QGROUP, slot_count, BLOCK, head_dim)
    list_groups = block_list.reshape(groups, QGROUP, slot_count)
    block_numbers = first_block + jnp.arange(blocks_dev, dtype=jnp.int32)
    block_groups = jnp.broadcast_to(block_numbers[None, :], (heads_local, blocks_dev)).reshape(
        groups, QGROUP
    )
    result = lax.map(
        attend_block, (query_heads, key_groups, value_groups, list_groups, block_groups)
    )
    result = result.reshape(heads_local, blocks_dev * BLOCK, head_dim).transpose(1, 0, 2)
    result = result.reshape(blocks_dev * BLOCK, heads_local * head_dim)
    return lax.all_to_all(result, "uly", split_axis=0, concat_axis=1, tiled=True)


def place(device, nu, nb):
    u, b = divmod(device, nb)
    return (u % 2 * (nu // 2) + u // 2) * nb + b


def lane_of(shape):
    return lax.broadcasted_iota(jnp.int32, shape, len(shape) - 1)


def pack_kernel(nb, q_hbm, k_hbm, v_hbm, list_hbm, out_hbm, *rest):
    bias_refs, (qkv, listed, packed, bias, in_sems, out_sems, list_sem) = rest[:nb], rest[nb:]
    rows, width = q_hbm.shape
    half, hd = rows // 2, LANES // 2
    pieces = in_sems.shape[0]
    wide, part = width // pieces, out_hbm.shape[1] // pieces
    low = lane_of((rows, LANES)) < hd
    low_half = lane_of((half, LANES)) < hd
    reads, writes = [], []
    for piece in range(pieces):
        cols = pl.ds(piece * wide, wide)
        reads.append(
            [
                pltpu.make_async_copy(
                    ref.at[:, cols], qkv.at[at, :, cols], in_sems.at[piece, at]
                )
                for at, ref in enumerate((q_hbm, k_hbm, v_hbm))
            ]
        )
        for copy in reads[-1]:
            copy.start()
    list_read = pltpu.make_async_copy(list_hbm, listed, list_sem)
    list_read.start()
    for piece in range(pieces):
        for copy in reads[piece]:
            copy.wait()
        for pair in range(piece * wide // LANES, (piece + 1) * wide // LANES):
            cols = slice(pair * LANES, (pair + 1) * LANES)
            q, k, v = qkv[0, :, cols], qkv[1, :, cols], qkv[2, :, cols]
            k_turned, v_turned = pltpu.roll(k, hd, 1), pltpu.roll(v, hd, 1)
            q_turned = pltpu.roll(q, hd, 1)
            for odd in range(2):
                u, b = divmod(2 * pair + odd, nb)
                if odd:
                    kv = jnp.where(low, k_turned, v)
                    qq = jnp.where(low_half, q_turned[:half], q[half:])
                else:
                    kv = jnp.where(low, k, v_turned)
                    qq = jnp.where(low_half, q[:half], q_turned[half:])
                packed[u % 2, u // 2, b, :rows, :] = kv
                packed[u % 2, u // 2, b, rows:, :] = qq
        some = pl.ds(piece * part, part)
        writes.append(
            pltpu.make_async_copy(packed.at[:, some], out_hbm.at[:, some], out_sems.at[piece])
        )
        writes[-1].start()
    list_read.wait()
    slots = listed[...]
    lane = lane_of((slots.shape[0], LANES)) - hd
    allowed = jnp.zeros((slots.shape[0], LANES), jnp.bool_)
    for slot in range(slots.shape[1]):
        allowed = allowed | (slots[:, slot : slot + 1] == lane)
    blocks = slots.shape[0] // nb
    all_bias = jnp.where(allowed, 0.0, NEG)
    for head in range(nb):
        bias[head] = all_bias[head * blocks : (head + 1) * blocks]
    me = lax.axis_index("blk")
    for step in range(nb):
        bias_refs[step][...] = bias[lax.rem(me + step, nb)]
    for copy in writes:
        copy.wait()


def attend_kernel(nu, nb, scale, g_ref, *rest):
    bias_refs, (out_ref, qx, kx, vt, bias) = rest[:nb], rest[nb:]
    chunks, packed, _ = g_ref.shape
    rows = packed * 2 // 3
    half, hd = rows // 2, LANES // 2
    blocks = chunks * rows // BLOCK
    here = blocks // nb
    me = lax.axis_index("blk")
    for step in range(nb):
        bias[lax.rem(me + nb - step, nb)] = bias_refs[step][...]
    lane = lane_of((rows, LANES))
    low = lane < hd
    low_half = lane_of((half, LANES)) < hd
    group = QGROUP * BLOCK
    each = group // rows
    mid = group // 2
    ones = vt.shape[0] - hd
    vt[:ones, :] = jnp.ones((ones, vt.shape[1]), jnp.bfloat16)

    def owner(t):
        return place(t % nu * nb + t // nu, nu, nb)

    def prepare(g):
        for t in range(g * each, (g + 1) * each):
            b = t * rows // BLOCK
            kv = g_ref[owner(t), :rows, :]
            q = g_ref[owner(t), rows:, :]
            row = jnp.broadcast_to(bias[b // here, b % here : b % here + 1, :], (half, LANES))
            row = row.astype(jnp.bfloat16)
            kx[t * rows : (t + 1) * rows, :] = jnp.where(low, kv, (lane == hd + b).astype(jnp.bfloat16))
            at = t // each * group + t % each * half
            qx[at : at + half, :] = jnp.where(low_half, q, row)
            qx[at + mid : at + mid + half, :] = jnp.where(low_half, pltpu.roll(q, hd, 1), row)
        for b in range(g * QGROUP, (g + 1) * QGROUP):
            pair = jnp.concatenate([g_ref[owner(b * BLOCK // rows + i), :rows, :] for i in range(BLOCK // rows)], axis=0)
            vt[ones:, b * BLOCK : (b + 1) * BLOCK] = pair.T[hd:, :]
    key = lax.broadcasted_iota(jnp.int32, (group, group), 0)
    col = lax.broadcasted_iota(jnp.int32, (group, group), 1)
    token = col % mid // half * rows + col // mid * half + col % half
    later = key > token
    factor = scale * math.log2(math.e)
    held = {}
    def score(slot, g, c, e, top):
        s = lax.dot_general(
            kx[c * group : e * group, :],
            qx[g * group : (g + 1) * group, :],
            (((1,), (1,)), ((), ())),
            preferred_element_type=jnp.float32,
        )
        for t in range(c, e):
            tile = s[(t - c) * group : (t - c + 1) * group]
            if t == g:
                tile = jnp.where(later, NEG, tile)
            held[slot, t] = tile
            m = jnp.max(tile.reshape(group // 8, 8, group), axis=0)
            top = m if top is None else jnp.maximum(top, m)
        return top
    def weigh(slot, c, top):
        s = held[slot, c]
        held[slot, c] = jnp.exp2((s - top) * factor).astype(jnp.bfloat16)
    def gather(slot, c0, c1, total):
        part = jnp.dot(
            vt[:, c0 * group : c1 * group], jnp.concatenate([held[slot, x] for x in range(c0, c1)], axis=0),
            preferred_element_type=jnp.float32,
        )
        return part if total is None else total + part
    def finish(g, total):
        result = (total[ones:].reshape(hd // 8, 8, group) * (1.0 / total[:8])[None]).reshape(hd, group)
        pair = jnp.concatenate([result[:, :mid], result[:, mid:]], axis=0)
        chunk = pair.T.astype(jnp.bfloat16)
        for i in range(each):
            out_ref[owner(g * each + i)] = chunk[i * half : (i + 1) * half]
    ready = set()
    def need(g):
        for i in range(g + 1):
            if i not in ready:
                ready.add(i); prepare(i)
    n = blocks // QGROUP
    order = list(range(1, n, 2)) + list(range(0, n, 2))[::-1]
    tops, slots = {}, AHEAD + 1
    for i in range(n + AHEAD):
        g = order[i] if i < n else None
        w = order[i - AHEAD] if i >= AHEAD else None
        a = [] if g is None else list(range(g + 1))
        b = [] if w is None else list(range(w + 1))
        if g is not None: need(g)
        top, total, done = None, None, 0
        k = 0
        for j in range(max(len(a), len(b))):
            while k < len(b) and (not a or k * len(a) <= j * len(b)):
                weigh((i - AHEAD) % slots, b[k], tops[w])
                k += 1
            if j < len(a) and j % 2 == 0:
                top = score(i % slots, g, j, min(j + 2, len(a)), top)
        while k < len(b):
            weigh((i - AHEAD) % slots, b[k], tops[w]); k += 1
        if g is not None:
            tops[g] = jnp.max(top, axis=0, keepdims=True)
        if w is not None:
            finish(w, gather((i - AHEAD) % slots, 0, w + 1, None))


def unpack_kernel(nu, nb, g_ref, out_hbm, out, sems):
    half, hd = g_ref.shape[1], LANES // 2
    low = lane_of((half, LANES)) < hd
    pieces = sems.shape[0]
    wide = out.shape[1] // pieces
    writes = []
    for piece in range(pieces):
        for pair in range(piece * wide // LANES, (piece + 1) * wide // LANES):
            cols = slice(pair * LANES, (pair + 1) * LANES)
            a, b = (g_ref[place(2 * pair + odd, nu, nb)] for odd in range(2))
            out[:half, cols] = jnp.where(low, a, pltpu.roll(b, hd, 1))
            out[half:, cols] = jnp.where(low, pltpu.roll(a, hd, 1), b)
        cols = pl.ds(piece * wide, wide)
        writes.append(
            pltpu.make_async_copy(out.at[:, cols], out_hbm.at[:, cols], sems.at[piece])
        )
        writes[-1].start()
    for copy in writes:
        copy.wait()


def exchange(chunks, nu, nb):
    order = [u * nb + b for odd in range(2) for u in range(odd, nu, 2) for b in range(nb)]
    return lax.all_to_all(chunks, EVERY, split_axis=0, concat_axis=0, axis_index_groups=[order])


def in_vmem(x):
    return pltpu.with_memory_space_constraint(x, pltpu.VMEM)


def by_head(queries, keys, values, block_list):
    nu, nb = lax.axis_size("uly"), lax.axis_size("blk")
    count = nu * nb
    rows, width = queries.shape
    heads_local, here, slots = block_list.shape
    head_dim = width // (heads_local * nu)
    blocks = here * nb
    vmem = pl.BlockSpec(memory_space=pltpu.VMEM)
    small = pltpu.VMEM((here, LANES), jnp.float32)
    anywhere = pl.BlockSpec(memory_space=pl.ANY)
    pieces = math.gcd(nu // 2, PIECES)
    laid = (2, nu // 2, nb, rows * 3 // 2, LANES)
    packed, *bias = pl.pallas_call(
        functools.partial(pack_kernel, nb),
        out_shape=(jax.ShapeDtypeStruct(laid, jnp.bfloat16),)
        + (small,) * nb,
        in_specs=[anywhere] * 4,
        out_specs=(anywhere,) + (vmem,) * nb,
        scratch_shapes=[
            pltpu.VMEM((3, rows, width), jnp.bfloat16),
            pltpu.VMEM((heads_local * here, slots), jnp.int32),
            pltpu.VMEM(laid, jnp.bfloat16),
            pltpu.VMEM((nb, here, LANES), jnp.float32),
            pltpu.SemaphoreType.DMA((pieces, 3)),
            pltpu.SemaphoreType.DMA((pieces,)),
            pltpu.SemaphoreType.DMA,
        ],
        cost_estimate=pl.CostEstimate(
            flops=4 * rows * width, bytes_accessed=12 * rows * width, transcendentals=0
        ),
    )(queries, keys, values, block_list.reshape(heads_local * here, slots))
    whole = exchange(packed.reshape(count, rows * 3 // 2, LANES), nu, nb)
    moved = [bias[0]] + [
        lax.ppermute(bias[step], "blk", [(i, (i + step) % nb) for i in range(nb)])
        for step in range(1, nb)
    ]
    tokens = count * rows
    attended = pl.pallas_call(
        functools.partial(attend_kernel, nu, nb, head_dim**-0.5),
        out_shape=pltpu.VMEM((count, rows // 2, LANES), jnp.bfloat16),
        in_specs=[vmem] * (nb + 1),
        out_specs=vmem,
        scratch_shapes=[
            pltpu.VMEM((tokens, LANES), jnp.bfloat16),
            pltpu.VMEM((tokens, LANES), jnp.bfloat16),
            pltpu.VMEM((head_dim + ONES, tokens), jnp.bfloat16),
            pltpu.VMEM((nb, here, LANES), jnp.float32),
        ],
        cost_estimate=pl.CostEstimate(
            flops=4 * tokens * tokens // 2 * LANES,
            bytes_accessed=4 * tokens * LANES * 2,
            transcendentals=tokens * tokens // 2,
        ),
    )(*(in_vmem(x) for x in (whole, *moved)))
    back = exchange(attended, nu, nb)
    return pl.pallas_call(
        functools.partial(unpack_kernel, nu, nb),
        out_shape=jax.ShapeDtypeStruct((rows, width), jnp.bfloat16),
        in_specs=[vmem],
        out_specs=anywhere,
        scratch_shapes=[
            pltpu.VMEM((rows, width), jnp.bfloat16),
            pltpu.SemaphoreType.DMA((pieces,)),
        ],
        cost_estimate=pl.CostEstimate(
            flops=2 * rows * width, bytes_accessed=4 * rows * width, transcendentals=0
        ),
    )(in_vmem(back))


def local(queries, keys, values, block_list):
    nu, nb = lax.axis_size("uly"), lax.axis_size("blk")
    rows, width = queries.shape
    heads_local, here, _ = block_list.shape
    head_dim = width // (heads_local * nu)
    blocks = here * nb
    one_head = (
        heads_local == nb
        and nu % 2 == 0
        and 2 * head_dim == LANES
        and blocks <= LANES // 2
        and blocks % QGROUP == 0
        and BLOCK % rows == 0
        and rows % 32 == 0
    )
    return (by_head if one_head else by_context)(queries, keys, values, block_list)


def solution(mesh):
    placed = (
        P(("blk", "uly"), None),
        P(("blk", "uly"), None),
        P(("blk", "uly"), None),
        P("uly", "blk", None),
    )
    return jax.shard_map(
        local, mesh=mesh, in_specs=placed, out_specs=P(("blk", "uly"), None), check_vma=False
    )
```

```python
import functools
import math

import jax
import jax.numpy as jnp
from jax import lax
from jax.experimental import pallas as pl
from jax.experimental.pallas import tpu as pltpu
from jax.sharding import PartitionSpec as P

BLOCK = 128
QGROUP = 2
LANES = 128
NEG = -1e30
ONES = 16
AHEAD = 2
PIECES = 2
EVERY = ("uly", "blk")


def head_major(token_rows, heads_local, head_dim):
    return token_rows.reshape(token_rows.shape[0] // BLOCK, BLOCK, heads_local, head_dim).transpose(
        2, 0, 1, 3
    )


def select_blocks(source, chosen):
    return jnp.take(source, chosen, axis=0)


def attend_block(operand):
    query_group, key_slots, value_slots, chosen, query_block = operand
    scale = query_group.shape[-1] ** (-0.5)
    scores = (
        jnp.einsum("abd,asjd->absj", query_group, key_slots, preferred_element_type=jnp.float32)
        * scale
    )
    positions = jnp.arange(BLOCK, dtype=jnp.int32)
    query_pos = query_block[:, None] * BLOCK + positions[None, :]
    key_pos = jnp.maximum(chosen, 0)[:, :, None] * BLOCK + positions[None, None, :]
    allowed = (chosen[:, None, :, None] >= 0) & (
        key_pos[:, None, :, :] <= query_pos[:, :, None, None]
    )
    scores = jnp.where(allowed, scores, -1e30)
    row_max = jnp.max(scores, axis=(2, 3), keepdims=True)
    weights = jnp.where(allowed, jnp.exp(scores - row_max), 0.0)
    denominator = jnp.sum(weights, axis=(2, 3))
    rounded = weights.astype(jnp.bfloat16)
    summed = jnp.einsum("absj,asjd->abd", rounded, value_slots, preferred_element_type=jnp.float32)
    return (summed / denominator[:, :, None]).astype(jnp.bfloat16)


def by_context(queries, keys, values, block_list):
    heads_local = block_list.shape[0]
    blocks_dev = block_list.shape[1]
    slot_count = block_list.shape[2]
    head_dim = queries.shape[1] // (heads_local * lax.axis_size("uly"))
    first_block = lax.axis_index("blk") * blocks_dev
    query_rows, key_rows, value_rows = (
        lax.all_to_all(queries, "uly", split_axis=1, concat_axis=0, tiled=True),
        lax.all_to_all(keys, "uly", split_axis=1, concat_axis=0, tiled=True),
        lax.all_to_all(values, "uly", split_axis=1, concat_axis=0, tiled=True),
    )
    keys_all = lax.all_gather(key_rows, "blk", axis=0, tiled=True)
    values_all = lax.all_gather(value_rows, "blk", axis=0, tiled=True)
    chosen = jnp.maximum(block_list, 0)
    key_slots = jax.vmap(select_blocks)(head_major(keys_all, heads_local, head_dim), chosen)
    value_slots = jax.vmap(select_blocks)(head_major(values_all, heads_local, head_dim), chosen)
    groups = heads_local * blocks_dev // QGROUP
    query_heads = head_major(query_rows, heads_local, head_dim).reshape(
        groups, QGROUP, BLOCK, head_dim
    )
    key_groups = key_slots.reshape(groups, QGROUP, slot_count, BLOCK, head_dim)
    value_groups = value_slots.reshape(groups, QGROUP, slot_count, BLOCK, head_dim)
    list_groups = block_list.reshape(groups, QGROUP, slot_count)
    block_numbers = first_block + jnp.arange(blocks_dev, dtype=jnp.int32)
    block_groups = jnp.broadcast_to(block_numbers[None, :], (heads_local, blocks_dev)).reshape(
        groups, QGROUP
    )
    result = lax.map(
        attend_block, (query_heads, key_groups, value_groups, list_groups, block_groups)
    )
    result = result.reshape(heads_local, blocks_dev * BLOCK, head_dim).transpose(1, 0, 2)
    result = result.reshape(blocks_dev * BLOCK, heads_local * head_dim)
    return lax.all_to_all(result, "uly", split_axis=0, concat_axis=1, tiled=True)


def place(device, nu, nb):
    u, b = divmod(device, nb)
    return (u % 2 * (nu // 2) + u // 2) * nb + b


def lane_of(shape):
    return lax.broadcasted_iota(jnp.int32, shape, len(shape) - 1)


def pack_kernel(nb, q_hbm, k_hbm, v_hbm, list_hbm, out_hbm, *rest):
    bias_refs, (qkv, listed, packed, bias, in_sems, out_sems, list_sem) = rest[:nb], rest[nb:]
    rows, width = q_hbm.shape
    half, hd = rows // 2, LANES // 2
    pieces = in_sems.shape[0]
    wide, part = width // pieces, out_hbm.shape[1] // pieces
    low = lane_of((rows, LANES)) < hd
    low_half = lane_of((half, LANES)) < hd
    reads, writes = [], []
    for piece in range(pieces):
        cols = pl.ds(piece * wide, wide)
        reads.append(
            [
                pltpu.make_async_copy(
                    ref.at[:, cols], qkv.at[at, :, cols], in_sems.at[piece, at]
                )
                for at, ref in enumerate((q_hbm, k_hbm, v_hbm))
            ]
        )
        for copy in reads[-1]:
            copy.start()
    list_read = pltpu.make_async_copy(list_hbm, listed, list_sem)
    list_read.start()
    for piece in range(pieces):
        for copy in reads[piece]:
            copy.wait()
        for pair in range(piece * wide // LANES, (piece + 1) * wide // LANES):
            cols = slice(pair * LANES, (pair + 1) * LANES)
            q, k, v = qkv[0, :, cols], qkv[1, :, cols], qkv[2, :, cols]
            k_turned, v_turned = pltpu.roll(k, hd, 1), pltpu.roll(v, hd, 1)
            q_turned = pltpu.roll(q, hd, 1)
            for odd in range(2):
                u, b = divmod(2 * pair + odd, nb)
                if odd:
                    kv = jnp.where(low, k_turned, v)
                    qq = jnp.where(low_half, q_turned[:half], q[half:])
                else:
                    kv = jnp.where(low, k, v_turned)
                    qq = jnp.where(low_half, q[:half], q_turned[half:])
                packed[u % 2, u // 2, b, :rows, :] = kv
                packed[u % 2, u // 2, b, rows:, :] = qq
        some = pl.ds(piece * part, part)
        writes.append(
            pltpu.make_async_copy(packed.at[:, some], out_hbm.at[:, some], out_sems.at[piece])
        )
        writes[-1].start()
    list_read.wait()
    slots = listed[...]
    lane = lane_of((slots.shape[0], LANES)) - hd
    allowed = jnp.zeros((slots.shape[0], LANES), jnp.bool_)
    for slot in range(slots.shape[1]):
        allowed = allowed | (slots[:, slot : slot + 1] == lane)
    blocks = slots.shape[0] // nb
    all_bias = jnp.where(allowed, 0.0, NEG)
    for head in range(nb):
        bias[head] = all_bias[head * blocks : (head + 1) * blocks]
    me = lax.axis_index("blk")
    for step in range(nb):
        bias_refs[step][...] = bias[lax.rem(me + step, nb)]
    for copy in writes:
        copy.wait()


def attend_kernel(nu, nb, scale, g_ref, *rest):
    bias_refs, (out_ref, qx, kx, vt, bias) = rest[:nb], rest[nb:]
    chunks, packed, _ = g_ref.shape
    rows = packed * 2 // 3
    half, hd = rows // 2, LANES // 2
    blocks = chunks * rows // BLOCK
    here = blocks // nb
    me = lax.axis_index("blk")
    for step in range(nb):
        bias[lax.rem(me + nb - step, nb)] = bias_refs[step][...]
    lane = lane_of((rows, LANES))
    low = lane < hd
    low_half = lane_of((half, LANES)) < hd
    group = QGROUP * BLOCK
    each = group // rows
    mid = group // 2
    ones = vt.shape[0] - hd
    vt[:ones, :] = jnp.ones((ones, vt.shape[1]), jnp.bfloat16)

    def owner(t):
        return place(t % nu * nb + t // nu, nu, nb)

    def prepare(g):
        for t in range(g * each, (g + 1) * each):
            b = t * rows // BLOCK
            kv = g_ref[owner(t), :rows, :]
            q = g_ref[owner(t), rows:, :]
            row = jnp.broadcast_to(bias[b // here, b % here : b % here + 1, :], (half, LANES))
            row = row.astype(jnp.bfloat16)
            kx[t * rows : (t + 1) * rows, :] = jnp.where(low, kv, (lane == hd + b).astype(jnp.bfloat16))
            at = t // each * group + t % each * half
            qx[at : at + half, :] = jnp.where(low_half, q, row)
            qx[at + mid : at + mid + half, :] = jnp.where(low_half, pltpu.roll(q, hd, 1), row)
        for b in range(g * QGROUP, (g + 1) * QGROUP):
            pair = jnp.concatenate([g_ref[owner(b * BLOCK // rows + i), :rows, :] for i in range(BLOCK // rows)], axis=0)
            vt[ones:, b * BLOCK : (b + 1) * BLOCK] = pair.T[hd:, :]
    key = lax.broadcasted_iota(jnp.int32, (group, group), 0)
    col = lax.broadcasted_iota(jnp.int32, (group, group), 1)
    token = col % mid // half * rows + col // mid * half + col % half
    later = key > token
    factor = scale * math.log2(math.e)
    held = {}
    def score(slot, g, c, e, top):
        s = lax.dot_general(
            kx[c * group : e * group, :],
            qx[g * group : (g + 1) * group, :],
            (((1,), (1,)), ((), ())),
            preferred_element_type=jnp.float32,
        )
        for t in range(c, e):
            tile = s[(t - c) * group : (t - c + 1) * group]
            if t == g:
                tile = jnp.where(later, NEG, tile)
            held[slot, t] = tile
            m = jnp.max(tile.reshape(group // 8, 8, group), axis=0)
            top = m if top is None else jnp.maximum(top, m)
        return top
    def weigh(slot, c, top):
        s = held[slot, c]
        held[slot, c] = jnp.exp2((s - top) * factor).astype(jnp.bfloat16)
    def gather(slot, c0, c1, total):
        part = jnp.dot(
            vt[:, c0 * group : c1 * group], jnp.concatenate([held[slot, x] for x in range(c0, c1)], axis=0),
            preferred_element_type=jnp.float32,
        )
        return part if total is None else total + part
    def finish(g, total):
        result = (total[ones:].reshape(hd // 8, 8, group) * (1.0 / total[:8])[None]).reshape(hd, group)
        pair = jnp.concatenate([result[:, :mid], result[:, mid:]], axis=0)
        chunk = pair.T.astype(jnp.bfloat16)
        for i in range(each):
            out_ref[owner(g * each + i)] = chunk[i * half : (i + 1) * half]
    ready = set()
    def need(g):
        for i in range(g + 1):
            if i not in ready:
                ready.add(i); prepare(i)
    n = blocks // QGROUP
    order = list(range(1, n, 2)) + list(range(0, n, 2))[::-1]
    tops, slots = {}, AHEAD + 1
    for i in range(n + AHEAD):
        g = order[i] if i < n else None
        w = order[i - AHEAD] if i >= AHEAD else None
        a = [] if g is None else list(range(g + 1))
        b = [] if w is None else list(range(w + 1))
        if g is not None: need(g)
        top, total, done = None, None, 0
        k = 0
        for j in range(max(len(a), len(b))):
            while k < len(b) and (not a or k * len(a) <= j * len(b)):
                weigh((i - AHEAD) % slots, b[k], tops[w])
                k += 1
            if j < len(a) and j % 2 == 0:
                top = score(i % slots, g, j, min(j + 2, len(a)), top)
        while k < len(b):
            weigh((i - AHEAD) % slots, b[k], tops[w]); k += 1
        if g is not None:
            tops[g] = jnp.max(top, axis=0, keepdims=True)
        if w is not None:
            finish(w, gather((i - AHEAD) % slots, 0, w + 1, None))


def unpack_kernel(nu, nb, g_ref, out_ref):
    half, hd = g_ref.shape[1], LANES // 2
    low = lane_of((half, LANES)) < hd
    for pair in range(out_ref.shape[1] // LANES):
        cols = slice(pair * LANES, (pair + 1) * LANES)
        a, b = (g_ref[place(2 * pair + odd, nu, nb)] for odd in range(2))
        out_ref[:half, cols] = jnp.where(low, a, pltpu.roll(b, hd, 1))
        out_ref[half:, cols] = jnp.where(low, pltpu.roll(a, hd, 1), b)


def exchange(chunks, nu, nb):
    order = [u * nb + b for odd in range(2) for u in range(odd, nu, 2) for b in range(nb)]
    return lax.all_to_all(chunks, EVERY, split_axis=0, concat_axis=0, axis_index_groups=[order])


def in_vmem(x):
    return pltpu.with_memory_space_constraint(x, pltpu.VMEM)


def by_head(queries, keys, values, block_list):
    nu, nb = lax.axis_size("uly"), lax.axis_size("blk")
    count = nu * nb
    rows, width = queries.shape
    heads_local, here, slots = block_list.shape
    head_dim = width // (heads_local * nu)
    blocks = here * nb
    vmem = pl.BlockSpec(memory_space=pltpu.VMEM)
    small = pltpu.VMEM((here, LANES), jnp.float32)
    anywhere = pl.BlockSpec(memory_space=pl.ANY)
    pieces = math.gcd(nu // 2, PIECES)
    laid = (2, nu // 2, nb, rows * 3 // 2, LANES)
    packed, *bias = pl.pallas_call(
        functools.partial(pack_kernel, nb),
        out_shape=(jax.ShapeDtypeStruct(laid, jnp.bfloat16),)
        + (small,) * nb,
        in_specs=[anywhere] * 4,
        out_specs=(anywhere,) + (vmem,) * nb,
        scratch_shapes=[
            pltpu.VMEM((3, rows, width), jnp.bfloat16),
            pltpu.VMEM((heads_local * here, slots), jnp.int32),
            pltpu.VMEM(laid, jnp.bfloat16),
            pltpu.VMEM((nb, here, LANES), jnp.float32),
            pltpu.SemaphoreType.DMA((pieces, 3)),
            pltpu.SemaphoreType.DMA((pieces,)),
            pltpu.SemaphoreType.DMA,
        ],
        cost_estimate=pl.CostEstimate(
            flops=4 * rows * width, bytes_accessed=12 * rows * width, transcendentals=0
        ),
    )(queries, keys, values, block_list.reshape(heads_local * here, slots))
    whole = exchange(packed.reshape(count, rows * 3 // 2, LANES), nu, nb)
    moved = [bias[0]] + [
        lax.ppermute(bias[step], "blk", [(i, (i + step) % nb) for i in range(nb)])
        for step in range(1, nb)
    ]
    tokens = count * rows
    attended = pl.pallas_call(
        functools.partial(attend_kernel, nu, nb, head_dim**-0.5),
        out_shape=pltpu.VMEM((count, rows // 2, LANES), jnp.bfloat16),
        in_specs=[vmem] * (nb + 1),
        out_specs=vmem,
        scratch_shapes=[
            pltpu.VMEM((tokens, LANES), jnp.bfloat16),
            pltpu.VMEM((tokens, LANES), jnp.bfloat16),
            pltpu.VMEM((head_dim + ONES, tokens), jnp.bfloat16),
            pltpu.VMEM((nb, here, LANES), jnp.float32),
        ],
        cost_estimate=pl.CostEstimate(
            flops=4 * tokens * tokens // 2 * LANES,
            bytes_accessed=4 * tokens * LANES * 2,
            transcendentals=tokens * tokens // 2,
        ),
    )(*(in_vmem(x) for x in (whole, *moved)))
    back = exchange(attended, nu, nb)
    return pl.pallas_call(
        functools.partial(unpack_kernel, nu, nb),
        out_shape=jax.ShapeDtypeStruct((rows, width), jnp.bfloat16),
        in_specs=[vmem],
        out_specs=vmem,
        cost_estimate=pl.CostEstimate(
            flops=2 * rows * width, bytes_accessed=4 * rows * width, transcendentals=0
        ),
    )(in_vmem(back))


def local(queries, keys, values, block_list):
    nu, nb = lax.axis_size("uly"), lax.axis_size("blk")
    rows, width = queries.shape
    heads_local, here, _ = block_list.shape
    head_dim = width // (heads_local * nu)
    blocks = here * nb
    one_head = (
        heads_local == nb
        and nu % 2 == 0
        and 2 * head_dim == LANES
        and blocks <= LANES // 2
        and blocks % QGROUP == 0
        and BLOCK % rows == 0
        and rows % 32 == 0
    )
    return (by_head if one_head else by_context)(queries, keys, values, block_list)


def solution(mesh):
    placed = (
        P(("blk", "uly"), None),
        P(("blk", "uly"), None),
        P(("blk", "uly"), None),
        P("uly", "blk", None),
    )
    return jax.shard_map(
        local, mesh=mesh, in_specs=placed, out_specs=P(("blk", "uly"), None), check_vma=False
    )
```
